32 devices in a mesh: section: 2 (over y), dp: 4 (over z), tensor: 4 (over x, core).
Axes of the slice: x: 2, y: 2, z: 4, core: 2. Of those that a mesh axis runs over, the one named last changes fastest.
Arguments:
- tokens: bfloat16 [2048, 1088], P(('dp', 'tensor')), may hold values from -6 to 6
- lengths: int32 [16, 2, 4], P(('dp', 'tensor')), may hold values from 1 to 42, 64 in all within a row
- w_qkv: bfloat16 [2, 1088, 3264], P('section'), may hold values from -2 to 2, as said below
- w_out: bfloat16 [2, 1088, 1088], P('section'), may hold values from -0.375 to 0.375
- w_up: bfloat16 [2, 1088, 4352], P('section', None, 'tensor'), may hold values from -0.1875 to 0.1875
- up_bias: float32 [2, 4352], P('section', 'tensor'), may hold values from -3 to 3
- w_down: bfloat16 [2, 4352, 1088], P('section', 'tensor'), may hold values from -0.09375 to 0.09375
- gains: float32 [2, 2, 1088], P('section'), may hold values from 0.25 to 1.75
- biases: float32 [2, 6, 1088], P('section'), may hold values from -2.5 to 2.5
- cotangent: bfloat16 [2048, 1088], P(('dp', 'tensor')), may hold values from -6 to 6
Outputs:
- layer_outputs: bfloat16 [2, 2048, 1088], P('section', ('dp', 'tensor'))
- input_grads: bfloat16 [2, 2048, 1088], P('section', ('dp', 'tensor'))
- grad_w_qkv: float32 [2, 1088, 3264], P('section', ('dp', 'tensor'))
- grad_w_out: float32 [2, 1088, 1088], P('section', ('dp', 'tensor'))
- grad_gains: float32 [2, 2, 1088], P('section', None, ('dp', 'tensor'))
- grad_biases: float32 [2, 6, 1088], P('section', None, ('dp', 'tensor'))
- grad_w_up: float32 [2, 1088, 4352], P('section', None, 'tensor')
- grad_up_bias: float32 [2, 4352], P('section', 'tensor')
- grad_w_down: float32 [2, 4352, 1088], P('section', 'tensor')
The draws below stay inside these ranges and needn't reach their ends.
Inputs may be any that keep to these rules, and one draw needn't show every extreme that they name: Each device's rows of one micro-batch hold 4 whole sequences whose lengths sum to 64; the longest is 42. `w_qkv`: columns are queries, keys and values in that order.
All inputs are finite; a program needn't handle non-finite values.
Results may differ from the reference program's by a relative error of at most 0.025.
Values may be sent and summed in bfloat16 or wider, within the bound.
A program may use at most 192 MiB of HBM per device.

```python
import math
import jax
import jax.numpy as jnp
import numpy as np
from jax import lax

D = 1088
HEADS = 17
HEAD_DIM = 64
FF = 4352
ROWS_MB = 64
MICRO = 2
SEQS = 4
DEV_ST = 16
TOKENS = 2048
N_TENSOR = 4


def draw_w_qkv(key, part):
    base = jnp.clip(jax.random.normal(key, (2, D, 3 * D), jnp.float32), -4.0, 4.0) * D ** (-0.5)
    return base.astype(jnp.bfloat16)


def level_of(stream_key, extent, cuts, low, largest):
    level = 1.0
    for position, parts in cuts:
        steps = jax.random.uniform(jax.random.fold_in(jax.random.fold_in(stream_key, 6), position), (parts,), jnp.float32, low / len(cuts), largest / len(cuts))
        level = level * jnp.repeat(jnp.exp(steps), extent[position] // parts).reshape((-1,) + (1,) * (len(extent) - 1 - position))
    return level


def profile(count, total, most, lean):
    weights = [(1 << 20) // math.isqrt(rank ** lean) + 1 for rank in range(2, count + 1)]
    rest, counts = total - most - (count - 1), [1] * (count - 1)
    while rest > 0:
        movable = [i for i in range(count - 1) if counts[i] < most]
        mass, left = sum([weights[i] for i in movable]), rest
        for i in movable:
            extra = min(most - counts[i], max(1, left * weights[i] // mass), rest)
            counts[i] = counts[i] + extra
            rest = rest - extra
    return np.array([most] + counts)


def ragged(own_key, amount, total, limit, slope):
    if amount == 2:
        one = jax.random.randint(own_key, (), max(1, total - limit), min(limit, total - 1) + 1)
        return jnp.stack([one, total - one])
    tallies = jnp.asarray(profile(amount, total, limit, slope), jnp.int32)
    couples = (amount - 1) // 2
    donor, receiver = tallies[1:1 + 2 * couples:2], tallies[2:2 + 2 * couples:2]
    margin = jnp.minimum(donor - 1, limit - receiver)
    moved = jax.random.randint(jax.random.fold_in(own_key, 1), (couples,), 0, 1 << 20) % (margin + 1)
    tallies = tallies.at[1:1 + 2 * couples:2].set(donor - moved).at[2:2 + 2 * couples:2].set(receiver + moved)
    return tallies[jax.random.permutation(jax.random.fold_in(own_key, 2), amount)]


def bell_draw(stream_key, dims, spread, reach, cuts=(), kind=jnp.bfloat16):
    level = level_of(stream_key, dims, cuts, -0.22, 0.18) if cuts else 1.0
    entries = jax.random.normal(stream_key, dims, jnp.float32) * spread * level
    return jnp.minimum(jnp.maximum(entries, -reach), reach).astype(kind)


def setup_inputs(seed: int = 0) -> dict:
    seeds = jax.random.split(jax.random.key(seed), 11)
    tokens = bell_draw(seeds[0], (TOKENS, D), 1.0, 6.0, ((0, 16),))
    lengths = jax.vmap(lambda own: ragged(own, SEQS, ROWS_MB, 2 * ROWS_MB // 3, 2))(jax.random.split(seeds[1], DEV_ST * MICRO)).reshape((DEV_ST, MICRO, SEQS)).astype(jnp.int32)
    w_qkv = draw_w_qkv(jax.random.fold_in(seeds[10], 71), 0)
    w_out = bell_draw(seeds[3], (2, D, D), (D // 4) ** -0.5, 0.375, ((0, 2),))
    w_up = bell_draw(seeds[4], (2, D, FF), D ** -0.5, 0.1875, ((0, 2), (2, 4)))
    up_bias = bell_draw(seeds[5], (2, FF), 0.5, 3.0, ((0, 2), (1, 4)), jnp.float32)
    w_down = bell_draw(seeds[6], (2, FF, D), FF ** -0.5, 0.09375, ((0, 2), (1, 4)))
    gains = jnp.clip(1.0 + 0.15 * jax.random.normal(seeds[7], (2, 2, D), jnp.float32), 0.25, 1.75)
    biases = bell_draw(seeds[8], (2, 6, D), 0.4, 2.5, ((0, 2),), jnp.float32)
    cotangent = bell_draw(seeds[9], (TOKENS, D), 1.0, 6.0, ((0, 16),))
    return {"tokens": tokens, "lengths": lengths, "w_qkv": w_qkv, "w_out": w_out, "w_up": w_up, "up_bias": up_bias, "w_down": w_down, "gains": gains, "biases": biases, "cotangent": cotangent}


EPSILON = 1e-05
GELU_SCALE = math.sqrt(2.0 / math.pi)
GELU_CUBIC = 0.044715

def norm_rows(values):
    centre = values - lax.optimization_barrier(jnp.mean(values, axis=-1, keepdims=True))
    inverse = lax.rsqrt(lax.optimization_barrier(jnp.mean(centre * centre, axis=-1, keepdims=True)) + EPSILON)
    return (centre * inverse, inverse)

def norm_back(grad_normed, normed, inverse, gain):
    scaled = grad_normed * gain
    return (scaled - lax.optimization_barrier(jnp.mean(scaled, axis=-1, keepdims=True)) - normed * lax.optimization_barrier(jnp.mean(scaled * normed, axis=-1, keepdims=True))) * inverse

def gelu_tanh(values):
    return 0.5 * values * (1.0 + jnp.tanh(GELU_SCALE * (values + GELU_CUBIC * values * values * values)))

def gelu_slope(values):
    tangent = jnp.tanh(GELU_SCALE * (values + GELU_CUBIC * values * values * values))
    return 0.5 * (1.0 + tangent) + 0.5 * values * (1.0 - tangent * tangent) * GELU_SCALE * (1.0 + 3.0 * GELU_CUBIC * values * values)

def contract_rows(left, right):
    return lax.dot_general(left, right, (((0,), (0,)), ((), ())), preferred_element_type=jnp.float32)

def contract_cols(left, right):
    return lax.dot_general(left, right, (((1,), (1,)), ((), ())), preferred_element_type=jnp.float32)

def make_allowed(seq_lengths):
    ends = jnp.cumsum(seq_lengths.astype(jnp.int32))
    places = jnp.arange(ROWS_MB, dtype=jnp.int32)
    segment = lax.optimization_barrier(jnp.sum((places[:, None] >= ends[None, :]).astype(jnp.int32), axis=1))
    return (segment[:, None] == segment[None, :]) & (places[None, :] <= places[:, None])

def round_trip(values):
    return lax.optimization_barrier(values.astype(jnp.bfloat16)).astype(jnp.float32)

def head_split(values):
    return values.reshape(ROWS_MB, HEADS, HEAD_DIM).astype(jnp.float32)

def scores_of(queries, keys_all, allowed):
    scores = jnp.einsum('qhd,khd->hqk', head_split(queries), head_split(keys_all), precision=lax.Precision.HIGHEST) * HEAD_DIM ** (-0.5)
    return jnp.where(allowed[None], scores, -jnp.inf)

def forward(layer_in, seq_lengths, params):
    w_qkv, w_out, w_up, up_bias, w_down, gains, biases, up_parts, down_parts = params
    allowed = make_allowed(seq_lengths)
    inflow = layer_in.astype(jnp.float32)
    normed_one, inverse_one = norm_rows(inflow)
    normal_one = (normed_one * gains[0] + biases[0]).astype(jnp.bfloat16)
    projected = jnp.dot(normal_one, w_qkv, preferred_element_type=jnp.float32)
    queries = (projected[:, :D] + biases[1]).astype(jnp.bfloat16)
    keys_all = projected[:, D:2 * D].astype(jnp.bfloat16)
    values_all = (projected[:, 2 * D:] + biases[2]).astype(jnp.bfloat16)
    masked = scores_of(queries, keys_all, allowed)
    peak = lax.optimization_barrier(jnp.max(masked, axis=-1, keepdims=True))
    log_total = peak + jnp.log(lax.optimization_barrier(jnp.sum(jnp.exp(masked - peak), axis=-1, keepdims=True)))
    probs = jnp.exp(masked - log_total).astype(jnp.bfloat16)
    mixed = jnp.einsum('hqk,khd->qhd', probs.astype(jnp.float32), head_split(values_all), precision=lax.Precision.HIGHEST)
    mixed = mixed.reshape(ROWS_MB, D).astype(jnp.bfloat16)
    residual = inflow + jnp.dot(mixed, w_out, preferred_element_type=jnp.float32) + biases[3]
    normed_two, inverse_two = norm_rows(residual)
    normal_two = (normed_two * gains[1] + biases[4]).astype(jnp.bfloat16)
    hidden_pre = jnp.dot(normal_two, w_up, preferred_element_type=jnp.float32) + up_bias
    hidden = gelu_tanh(hidden_pre).astype(jnp.bfloat16)
    pieces = jnp.einsum('rjf,jfd->jrd', hidden.reshape(ROWS_MB, N_TENSOR, FF // N_TENSOR).astype(jnp.float32), down_parts, precision=lax.Precision.HIGHEST)
    branch = lax.optimization_barrier(jnp.sum(round_trip(pieces), axis=0))
    result = (residual + branch + biases[5]).astype(jnp.bfloat16)
    kept = (allowed, normal_one, normed_one, inverse_one, queries, keys_all, values_all, mixed, log_total, normed_two, inverse_two, normal_two, hidden_pre, hidden)
    return (result, kept)

def backward(grad_out, kept, params):
    w_qkv, w_out, w_up, up_bias, w_down, gains, biases, up_parts, down_parts = params
    allowed, normal_one, normed_one, inverse_one, queries, keys_all, values_all, mixed, log_total, normed_two, inverse_two, normal_two, hidden_pre, hidden = kept
    grad_flow = grad_out.astype(jnp.float32)
    grad_down = contract_rows(hidden, grad_out)
    grad_hidden = contract_cols(grad_out, w_down)
    grad_pre = grad_hidden * gelu_slope(hidden_pre)
    grad_up_bias = lax.optimization_barrier(jnp.sum(grad_pre, axis=0))
    grad_pre_b = grad_pre.astype(jnp.bfloat16)
    grad_up = contract_rows(normal_two, grad_pre_b)
    pieces = jnp.einsum('rjf,djf->jrd', grad_pre_b.reshape(ROWS_MB, N_TENSOR, FF // N_TENSOR).astype(jnp.float32), up_parts, precision=lax.Precision.HIGHEST)
    grad_two = lax.optimization_barrier(jnp.sum(round_trip(pieces), axis=0))
    grad_resid = grad_flow + norm_back(grad_two, normed_two, inverse_two, gains[1])
    grad_resid_b = grad_resid.astype(jnp.bfloat16)
    grad_wout = contract_rows(mixed, grad_resid_b)
    grad_mixed = contract_cols(grad_resid_b, w_out).astype(jnp.bfloat16)
    masked = scores_of(queries, keys_all, allowed)
    probs_f = jnp.exp(masked - log_total)
    probs_b = probs_f.astype(jnp.bfloat16).astype(jnp.float32)
    grad_heads = head_split(grad_mixed)
    grad_probs = jnp.einsum('qhd,khd->hqk', grad_heads, head_split(values_all), precision=lax.Precision.HIGHEST)
    grad_values = jnp.einsum('hqk,qhd->khd', probs_b, grad_heads, precision=lax.Precision.HIGHEST).reshape(ROWS_MB, D)
    centre = lax.optimization_barrier(jnp.sum(probs_f * grad_probs, axis=-1, keepdims=True))
    grad_scores = (probs_f * (grad_probs - centre) * HEAD_DIM ** (-0.5)).astype(jnp.bfloat16).astype(jnp.float32)
    grad_queries = jnp.einsum('hqk,khd->qhd', grad_scores, head_split(keys_all), precision=lax.Precision.HIGHEST).reshape(ROWS_MB, D)
    grad_keys = jnp.einsum('hqk,qhd->khd', grad_scores, head_split(queries), precision=lax.Precision.HIGHEST).reshape(ROWS_MB, D)
    grad_proj = jnp.concatenate([grad_queries, grad_keys, grad_values], axis=1).astype(jnp.bfloat16)
    grad_wqkv = contract_rows(normal_one, grad_proj)
    grad_one = contract_cols(grad_proj, w_qkv)
    grad_in = (grad_resid + norm_back(grad_one, normed_one, inverse_one, gains[0])).astype(jnp.bfloat16)
    gain_grads = jnp.stack([lax.optimization_barrier(jnp.sum(normed_one * grad_one, axis=0)), lax.optimization_barrier(jnp.sum(normed_two * grad_two, axis=0))])
    bias_grads = jnp.stack([lax.optimization_barrier(jnp.sum(grad_one, axis=0)), lax.optimization_barrier(jnp.sum(grad_queries, axis=0)), lax.optimization_barrier(jnp.sum(grad_values, axis=0)), lax.optimization_barrier(jnp.sum(grad_resid, axis=0)), lax.optimization_barrier(jnp.sum(grad_two, axis=0)), lax.optimization_barrier(jnp.sum(grad_flow, axis=0))])
    return (grad_in, (grad_wqkv, grad_wout, gain_grads, bias_grads, grad_up, grad_down, grad_up_bias))

def layer_params(layer, w_qkv, w_out, w_up, up_bias, w_down, gains, biases):
    up_parts = w_up[layer].astype(jnp.float32).reshape(D, N_TENSOR, FF // N_TENSOR)
    down_parts = w_down[layer].astype(jnp.float32).reshape(N_TENSOR, FF // N_TENSOR, D)
    return (w_qkv[layer], w_out[layer], w_up[layer], up_bias[layer], w_down[layer], gains[layer], biases[layer], up_parts, down_parts)

def run_layer(inputs, cots, seq_table, params):
    zeros_init = (jnp.zeros((D, 3 * D), jnp.float32), jnp.zeros((D, D), jnp.float32), jnp.zeros((2, D), jnp.float32), jnp.zeros((6, D), jnp.float32), jnp.zeros((D, FF), jnp.float32), jnp.zeros((FF, D), jnp.float32), jnp.zeros((FF,), jnp.float32))

    def one_block(totals, block):
        block_in, block_cot, block_lengths = block
        result, kept = forward(block_in, block_lengths, params)
        grad_in, grads = backward(block_cot, kept, params)
        return (jax.tree.map(jnp.add, totals, grads), (result, grad_in))
    return lax.scan(one_block, zeros_init, (inputs, cots, seq_table))

def reference(tokens, lengths, w_qkv, w_out, w_up, up_bias, w_down, gains, biases, cotangent):
    block_count = DEV_ST * MICRO
    inputs = tokens.reshape(block_count, ROWS_MB, D)
    cots = cotangent.reshape(block_count, ROWS_MB, D)
    seq_table = lengths.reshape(block_count, SEQS)
    first = layer_params(0, w_qkv, w_out, w_up, up_bias, w_down, gains, biases)
    second = layer_params(1, w_qkv, w_out, w_up, up_bias, w_down, gains, biases)
    middle = lax.map(lambda block: forward(block[0], block[1], first)[0], (inputs, seq_table))
    totals_two, (outputs_two, grads_mid) = run_layer(middle, cots, seq_table, second)
    totals_one, (unused_out, grads_in) = run_layer(inputs, grads_mid, seq_table, first)
    layer_outputs = jnp.stack([middle.reshape(TOKENS, D), outputs_two.reshape(TOKENS, D)])
    input_grads = jnp.stack([grads_in.reshape(TOKENS, D), grads_mid.reshape(TOKENS, D)])
    stacked = [jnp.stack([part_one, part_two]) for part_one, part_two in zip(totals_one, totals_two)]
    return (layer_outputs, input_grads, stacked[0], stacked[1], stacked[2], stacked[3], stacked[4], stacked[6], stacked[5])
```

```python
import functools
import math

import jax
import jax.numpy as jnp
from jax import lax
from jax.experimental import pallas as pl
from jax.experimental.pallas import tpu as pltpu
from jax.sharding import PartitionSpec as P

HEADS = 17
LANES = 128
EPSILON = 1e-05
GELU_SCALE = math.sqrt(2.0 / math.pi)
GELU_CUBIC = 0.044715
MESH = pl.DeviceIdType.MESH
BF = jnp.bfloat16
F32 = jnp.float32


def dot(left, right, left_dim=1, right_dim=0):
    return lax.dot_general(
        left, right, (((left_dim,), (right_dim,)), ((), ())), preferred_element_type=F32
    )


def norm_rows(values):
    centre = values - jnp.mean(values, axis=-1, keepdims=True)
    inverse = lax.rsqrt(jnp.mean(centre * centre, axis=-1, keepdims=True) + EPSILON)
    return (centre * inverse, inverse)


def norm_back(grad_normed, normed, inverse, gain):
    scaled = grad_normed * gain
    return (
        scaled
        - jnp.mean(scaled, axis=-1, keepdims=True)
        - normed * jnp.mean(scaled * normed, axis=-1, keepdims=True)
    ) * inverse


def gelu_both(values):
    square = values * values
    tangent = jnp.tanh(GELU_SCALE * values * (1.0 + GELU_CUBIC * square))
    raised = 0.5 * (1.0 + tangent)
    slope = raised + (0.5 * GELU_SCALE) * values * (1.0 - tangent * tangent) * (
        1.0 + 3.0 * GELU_CUBIC * square
    )
    return values * raised, slope


def layers_kernel(
    chips,
    chunks,
    tokens_ref,
    len_ref,
    wqkv_hbm,
    wout_hbm,
    wup_hbm,
    upb_ref,
    wdn_hbm,
    gains_ref,
    bias_ref,
    cot_ref,
    res_ref,
    gin_ref,
    one_ref,
    mix_ref,
    gproj_ref,
    gres_ref,
    two_ref,
    gown_ref,
    small_ref,
    wqkv,
    wout,
    wup,
    wdn,
    lin,
    x_all,
    g_all,
    hid,
    slope,
    gpre,
    ghid,
    q_s,
    k_s,
    v_s,
    gm_s,
    gq_s,
    probs,
    bias_s,
    n1_s,
    n2_s,
    inv_s,
    resid,
    gresid,
    acc,
    local_part,
    f_beside,
    f_besideb,
    f_mine,
    f_across,
    f_acrossb,
    b_beside,
    b_besideb,
    b_mine,
    b_across,
    b_acrossb,
    w_sem,
    y_send,
    y_recv,
    gx_send,
    gx_recv,
    gb_send,
    gb_recv,
    sx_send,
    sx_recv,
    sb_send,
    sb_recv,
):
    sec = lax.axis_index("section")
    me = lax.axis_index("tensor")
    core = lax.rem(me, 2)
    chip = me // 2
    partner = me + 1 - 2 * core
    hops = chips - 1
    up_chips = [lax.rem(chip + k, chips) for k in range(1, chips)]
    down_chips = [lax.rem(chip + chips - k, chips) for k in range(1, chips)]
    rows, width = tokens_ref.shape
    part_rows = rows // chunks
    hidden_width = wup.shape[1]
    heads_lane = LANES // (width // HEADS)
    head_width = width // HEADS
    pairs = -(-HEADS // heads_lane)
    scale = head_width ** (-0.5)

    loads = [
        pltpu.make_async_copy(src, dst, w_sem.at[i])
        for i, (src, dst) in enumerate(
            ((wqkv_hbm, wqkv), (wout_hbm, wout), (wup_hbm, wup), (wdn_hbm, wdn))
        )
    ]
    for load in loads:
        load.start()
    barrier = pltpu.get_barrier_semaphore()
    friends = [{"tensor": partner}, {"section": 1 - sec}]
    friends += [{"tensor": c * 2 + core} for c in up_chips]
    for friend in friends:
        pl.semaphore_signal(barrier, inc=1, device_id=friend, device_id_type=MESH)

    def remote(src, dst, send_sem, recv_sem, where):
        return pltpu.make_async_remote_copy(
            src_ref=src,
            dst_ref=dst,
            send_sem=send_sem,
            recv_sem=recv_sem,
            device_id=where,
            device_id_type=MESH,
        )

    def span(first, size):
        return pl.ds(pl.multiple_of(first, 16), size)

    blocks, seqs = len_ref.shape
    row_id = lax.broadcasted_iota(jnp.int32, (rows, rows), 0)
    col_id = lax.broadcasted_iota(jnp.int32, (rows, rows), 1)
    row_seg = jnp.zeros((rows, rows), jnp.int32)
    col_seg = jnp.zeros((rows, rows), jnp.int32)
    for b in range(blocks):
        end = b * (rows // blocks)
        for s in range(seqs):
            end = end + len_ref[b, s]
            row_seg += (row_id >= end).astype(jnp.int32)
            col_seg += (col_id >= end).astype(jnp.int32)
    allowed = (row_seg == col_seg) & (col_id <= row_id)
    bias_s[...] = jnp.where(allowed, 0.0, -jnp.inf).astype(F32)
    lane = lax.broadcasted_iota(jnp.int32, (rows, LANES), 1)

    def stacked(tile):
        zero = jnp.zeros_like(tile)
        return jnp.concatenate(
            [jnp.where(lane // head_width == j, tile, zero) for j in range(heads_lane)], axis=0
        )

    def unstacked(tile):
        out = tile[:rows]
        for j in range(1, heads_lane):
            out = jnp.where(lane // head_width == j, tile[j * rows : (j + 1) * rows], out)
        return out

    def lanes(p):
        return slice(p * LANES, (p + 1) * LANES)

    pl.semaphore_wait(barrier, len(friends))

    def gather_start(buf, which):
        base = me * rows
        for c in range(chunks):
            mine = buf.at[span(base + c * part_rows, part_rows)]
            for k in range(hops):
                i = k * chunks + c
                remote(
                    mine,
                    mine,
                    gx_send.at[which, i],
                    gx_recv.at[which, i],
                    {"tensor": up_chips[k] * 2 + core},
                ).start()
        mine = buf.at[span(base, rows)]
        last = hops * chunks
        remote(
            mine, mine, gb_send.at[which, last], gb_recv.at[which, last], {"tensor": partner}
        ).start()

    def from_chip(buf, k, c, whose):
        return buf.at[span((down_chips[k] * 2 + whose) * rows + c * part_rows, part_rows)]

    def gather_forward(buf, which, k, c):
        i = k * chunks + c
        came = from_chip(buf, k, c, core)
        remote(
            came, came, gx_send.at[which, i], gx_recv.at[which, i], {"tensor": partner}
        ).wait_recv()
        remote(
            came, came, gb_send.at[which, i], gb_recv.at[which, i], {"tensor": partner}
        ).start()

    def gather_arrived(buf, which, k, c):
        i = k * chunks + c
        came = from_chip(buf, k, c, 1 - core)
        remote(
            came, came, gb_send.at[which, i], gb_recv.at[which, i], {"tensor": partner}
        ).wait_recv()

    def gather_partner(buf, which):
        last = hops * chunks
        came = buf.at[span(partner * rows, rows)]
        remote(
            came, came, gb_send.at[which, last], gb_recv.at[which, last], {"tensor": partner}
        ).wait_recv()

    def gather_end(buf, which):
        base = me * rows
        mine = buf.at[span(base, rows)]
        some = buf.at[span(base, part_rows)]
        for i in range(hops * chunks):
            remote(
                some, some, gx_send.at[which, i], gx_recv.at[which, i], {"tensor": partner}
            ).wait_send()
            remote(
                some, some, gb_send.at[which, i], gb_recv.at[which, i], {"tensor": partner}
            ).wait_send()
        last = hops * chunks
        remote(
            mine, mine, gb_send.at[which, last], gb_recv.at[which, last], {"tensor": partner}
        ).wait_send()

    def ffn_pass(gathered, stage_one, stage_two, which, bufs, ready):
        beside, besideb, mine_s, across, acrossb = bufs
        order = [(k, c) for c in range(chunks) for k in range(hops)]
        chip_rows = [span(chip * 2 * rows, 2 * rows)]
        last = hops * chunks

        def both(k, c):
            theirs = down_chips[k] * 2 + 1 - core
            ours = down_chips[k] * 2 + core
            return [
                span(theirs * rows + c * part_rows, part_rows),
                span(ours * rows + c * part_rows, part_rows),
            ]

        if gathered is not None:
            buf, gwhich = gathered
            gather_partner(buf, gwhich)
            if stage_one is not None:
                stage_one(chip_rows)
            if order:
                gather_forward(buf, gwhich, *order[0])

        def local():
            value = stage_two(chip_rows)
            theirs = jnp.where(core == 0, value[rows:], value[:rows])
            ours = jnp.where(core == 0, value[:rows], value[rows:])
            beside[span(last * part_rows, rows)] = theirs.astype(BF)
            local_part[...] = ours
            remote(
                beside.at[span(last * part_rows, rows)],
                besideb.at[span(last * part_rows, rows)],
                sb_send.at[which, last],
                sb_recv.at[which, last],
                {"tensor": partner},
            ).start()

        for n, (k, c) in enumerate(order):
            i = k * chunks + c
            where = span(i * part_rows, part_rows)
            if gathered is not None:
                gather_arrived(buf, gwhich, k, c)
                if stage_one is not None:
                    stage_one(both(k, c))
            value = stage_two(both(k, c))
            beside[where] = value[:part_rows].astype(BF)
            mine_s[where] = value[part_rows:].astype(BF)
            pair = remote(
                beside.at[where],
                besideb.at[where],
                sb_send.at[which, i],
                sb_recv.at[which, i],
                {"tensor": partner},
            )
            pair.start()
            if gathered is not None and n + 1 < len(order):
                gather_forward(buf, gwhich, *order[n + 1])
            if n == 0:
                local()
            pair.wait_recv()
            across[where] = (mine_s[where].astype(F32) + besideb[where].astype(F32)).astype(BF)
            remote(
                across.at[where],
                acrossb.at[where],
                sx_send.at[which, i],
                sx_recv.at[which, i],
                {"tensor": down_chips[k] * 2 + core},
            ).start()
        if not order:
            local()
        where = span(last * part_rows, rows)
        final = remote(
            beside.at[where],
            besideb.at[where],
            sb_send.at[which, last],
            sb_recv.at[which, last],
            {"tensor": partner},
        )
        final.wait_recv()
        for c in range(chunks):
            here = slice(c * part_rows, (c + 1) * part_rows)
            total = local_part[here] + besideb[
                span(last * part_rows + c * part_rows, part_rows)
            ].astype(F32)
            for k in range(hops):
                i = k * chunks + c
                spot = span(i * part_rows, part_rows)
                remote(
                    across.at[spot],
                    acrossb.at[spot],
                    sx_send.at[which, i],
                    sx_recv.at[which, i],
                    {"tensor": partner},
                ).wait_recv()
                total = total + acrossb[spot].astype(F32)
            ready(c, here, total)
        final.wait_send()
        for k, c in order:
            i = k * chunks + c
            spot = span(i * part_rows, part_rows)
            remote(
                beside.at[spot],
                besideb.at[spot],
                sb_send.at[which, i],
                sb_recv.at[which, i],
                {"tensor": partner},
            ).wait_send()
            remote(
                across.at[spot],
                acrossb.at[spot],
                sx_send.at[which, i],
                sx_recv.at[which, i],
                {"tensor": partner},
            ).wait_send()

    def take(ref, spans):
        if len(spans) == 1:
            return ref[spans[0]]
        return jnp.concatenate([ref[s] for s in spans], axis=0)

    def put(ref, spans, value):
        size = value.shape[0] // len(spans)
        for n, s in enumerate(spans):
            ref[s] = value[n * size : (n + 1) * size].astype(ref.dtype)

    def up_stage(spans):
        pre = dot(take(x_all, spans), wup[...]) + upb_ref[...]
        value, lean = gelu_both(pre)
        put(hid, spans, value)
        put(slope, spans, lean)

    def grad_stage(spans):
        put(ghid, spans, dot(take(g_all, spans), wdn[...], 1, 1))

    def pre_stage(spans):
        put(gpre, spans, take(ghid, spans) * take(slope, spans).astype(F32))

    def down_part(spans):
        return dot(take(hid, spans), wdn[...])

    def up_back(spans):
        return dot(take(gpre, spans), wup[...], 1, 1)

    f_bufs = (f_beside, f_besideb, f_mine, f_across, f_acrossb)
    b_bufs = (b_beside, b_besideb, b_mine, b_across, b_acrossb)

    def result_ready(c, here, total):
        res_ref[here] = (resid[here] + total + bias_ref[5:6]).astype(BF)

    def y_copy(src, dst, i):
        return remote(src, dst, y_send.at[i], y_recv.at[i], {"section": 1 - sec})

    def result_send(c, here, total):
        result_ready(c, here, total)
        y_copy(res_ref.at[here], lin.at[here], c).start()

    def acc_ready(c, here, total):
        acc[here] = total

    own = span(me * rows, rows)

    @pl.when(sec == 1)
    def _():
        g_all[own] = cot_ref[...]
        gather_start(g_all, 1)
        loads[3].wait()
        gather_partner(g_all, 1)
        grad_stage([span(chip * 2 * rows, 2 * rows)])
        for c in range(chunks):
            for k in range(hops):
                gather_forward(g_all, 1, k, c)
                gather_arrived(g_all, 1, k, c)
        for k in range(hops):
            grad_stage([span(down_chips[k] * 2 * rows, 2 * rows)])
        gather_end(g_all, 1)
        for c in range(chunks):
            here = slice(c * part_rows, (c + 1) * part_rows)
            y_copy(res_ref.at[here], lin.at[here], c).wait_recv()

    @pl.when(sec == 0)
    def _():
        loads[3].wait()
        lin[...] = tokens_ref[...]

    normed, inverse = norm_rows(lin[...].astype(F32))
    n1_s[...] = normed
    inv_s[:, 0:1] = inverse
    one_ref[...] = (normed * gains_ref[0:1] + bias_ref[0:1]).astype(BF)
    loads[0].wait()
    proj = dot(one_ref[...], wqkv[...])
    for ref, first, shift in ((q_s, 0, 1), (k_s, width, None), (v_s, 2 * width, 2)):
        value = proj[:, first : first + width]
        if shift is not None:
            value = value + bias_ref[shift : shift + 1]
        ref[:, :width] = value.astype(BF)
        if ref.shape[1] > width:
            ref[:, width:] = jnp.zeros((rows, ref.shape[1] - width), BF)
    for p in range(pairs):
        probs[p] = dot(stacked(q_s[:, lanes(p)]), k_s[:, lanes(p)], 1, 1)
    limit = jnp.concatenate([bias_s[...]] * heads_lane, axis=0)
    for p in range(pairs):
        masked = probs[p] * scale + limit
        raised = jnp.exp(masked - jnp.max(masked, axis=-1, keepdims=True))
        probs[p] = raised / jnp.sum(raised, axis=-1, keepdims=True)
    for p in range(pairs):
        tile = unstacked(dot(probs[p].astype(BF), v_s[:, lanes(p)])).astype(BF)
        size = min(width - p * LANES, LANES)
        mix_ref[:, p * LANES : p * LANES + size] = tile[:, :size]
    loads[1].wait()
    value = lin[...].astype(F32) + dot(mix_ref[...], wout[...]) + bias_ref[3:4]
    resid[...] = value
    normed, inverse = norm_rows(value)
    n2_s[...] = normed
    inv_s[:, 1:2] = inverse
    two = (normed * gains_ref[1:2] + bias_ref[4:5]).astype(BF)
    two_ref[...] = two
    x_all[own] = two
    gather_start(x_all, 0)
    loads[2].wait()

    @pl.when(sec == 0)
    def _():
        ffn_pass((x_all, 0), up_stage, down_part, 0, f_bufs, result_send)
        for c in range(chunks):
            here = slice(c * part_rows, (c + 1) * part_rows)
            arrive = g_all.at[span(me * rows + c * part_rows, part_rows)]
            y_copy(res_ref.at[here], lin.at[here], c).wait_send()
            y_copy(gin_ref.at[here], arrive, c).wait_recv()
        gather_start(g_all, 1)

        def both_stages(spans):
            grad_stage(spans)
            pre_stage(spans)

        ffn_pass((g_all, 1), both_stages, up_back, 1, b_bufs, acc_ready)
        gather_end(g_all, 1)

    @pl.when(sec == 1)
    def _():
        def both_stages(spans):
            up_stage(spans)
            pre_stage(spans)

        ffn_pass((x_all, 0), both_stages, up_back, 1, b_bufs, acc_ready)

    gather_end(x_all, 0)

    gown_ref[...] = g_all[own]
    flow = g_all[own].astype(F32)
    grad_two = acc[...]
    normed = n2_s[...]
    value = flow + norm_back(grad_two, normed, inv_s[:, 1:2], gains_ref[1:2])
    gresid[...] = value
    gres_ref[...] = value.astype(BF)
    small_ref[1:2] = jnp.sum(normed * grad_two, axis=0, keepdims=True)
    small_ref[5:6] = jnp.sum(value, axis=0, keepdims=True)
    small_ref[6:7] = jnp.sum(grad_two, axis=0, keepdims=True)
    small_ref[7:8] = jnp.sum(flow, axis=0, keepdims=True)
    gm_s[:, :width] = dot(gres_ref[...], wout[...], 1, 1).astype(BF)
    if gm_s.shape[1] > width:
        gm_s[:, width:] = jnp.zeros((rows, gm_s.shape[1] - width), BF)
    for p in range(pairs):
        size = min(width - p * LANES, LANES)
        grads = stacked(gm_s[:, lanes(p)])
        weights = probs[p]
        grad_probs = dot(grads, v_s[:, lanes(p)], 1, 1)
        centre = jnp.sum(weights * grad_probs, axis=-1, keepdims=True)
        grad_scores = (weights * (grad_probs - centre) * scale).astype(BF)
        gv = dot(weights.astype(BF), grads, 0, 0)
        gq = unstacked(dot(grad_scores, k_s[:, lanes(p)]))
        gk = dot(grad_scores, stacked(q_s[:, lanes(p)]), 0, 0)
        at = p * LANES
        small_ref[3:4, at : at + size] = jnp.sum(gq, axis=0, keepdims=True)[:, :size]
        small_ref[4:5, at : at + size] = jnp.sum(gv, axis=0, keepdims=True)[:, :size]
        gproj_ref[:, at : at + size] = gq.astype(BF)[:, :size]
        gq_s[:, at : at + LANES] = gk.astype(BF)
        gproj_ref[:, 2 * width + at : 2 * width + at + size] = gv.astype(BF)[:, :size]
    gproj_ref[:, width : 2 * width] = gq_s[:, :width]
    grad_one = dot(gproj_ref[...], wqkv[...], 1, 1)
    normed = n1_s[...]
    gin_ref[...] = (
        gresid[...] + norm_back(grad_one, normed, inv_s[:, 0:1], gains_ref[0:1])
    ).astype(BF)

    @pl.when(sec == 1)
    def _():
        for c in range(chunks):
            here = slice(c * part_rows, (c + 1) * part_rows)
            arrive = g_all.at[span(me * rows + c * part_rows, part_rows)]
            y_copy(gin_ref.at[here], arrive, c).start()
        ffn_pass(None, None, down_part, 0, f_bufs, result_ready)
        for c in range(chunks):
            here = slice(c * part_rows, (c + 1) * part_rows)
            arrive = g_all.at[span(me * rows + c * part_rows, part_rows)]
            y_copy(gin_ref.at[here], arrive, c).wait_send()

    small_ref[0:1] = jnp.sum(normed * grad_one, axis=0, keepdims=True)
    small_ref[2:3] = jnp.sum(grad_one, axis=0, keepdims=True)


def run_layers(tokens, lengths, w_qkv, w_out, w_up, up_bias, w_down, gains, biases, cotangent):
    devices = lax.axis_size("tensor")
    chips = devices // 2
    hops = chips - 1
    rows, width = tokens.shape
    chunks = 2 if rows % 32 == 0 else 1
    part_rows = rows // chunks
    hidden = w_up.shape[1]
    padded = -(-width // LANES) * LANES
    heads_lane = LANES // (width // HEADS)
    pairs = -(-HEADS // heads_lane)
    group = devices * rows
    moved = hops * chunks * part_rows
    shape = jax.ShapeDtypeStruct
    vmem = pl.BlockSpec(memory_space=pltpu.VMEM)
    smem = pl.BlockSpec(memory_space=pltpu.SMEM)
    hbm = pl.BlockSpec(memory_space=pl.ANY)
    dma = pltpu.SemaphoreType.DMA
    bufs = [
        pltpu.VMEM((moved + rows, width), BF),
        pltpu.VMEM((moved + rows, width), BF),
        pltpu.VMEM((max(moved, 16), width), BF),
        pltpu.VMEM((max(moved, 16), width), BF),
        pltpu.VMEM((max(moved, 16), width), BF),
    ]
    count = hops * chunks + 1
    return pl.pallas_call(
        functools.partial(layers_kernel, chips, chunks),
        out_shape=(
            shape((rows, width), BF),
            shape((rows, width), BF),
            shape((rows, width), BF),
            shape((rows, width), BF),
            shape((rows, 3 * width), BF),
            shape((rows, width), BF),
            shape((rows, width), BF),
            shape((rows, width), BF),
            shape((8, width), F32),
        ),
        in_specs=[vmem, smem, hbm, hbm, hbm, vmem, hbm, vmem, vmem, vmem],
        out_specs=(vmem,) * 9,
        scratch_shapes=[
            pltpu.VMEM(w_qkv.shape, BF),
            pltpu.VMEM(w_out.shape, BF),
            pltpu.VMEM(w_up.shape, BF),
            pltpu.VMEM(w_down.shape, BF),
            pltpu.VMEM((rows, width), BF),
            pltpu.VMEM((group, width), BF),
            pltpu.VMEM((group, width), BF),
            pltpu.VMEM((group, hidden), BF),
            pltpu.VMEM((group, hidden), BF),
            pltpu.VMEM((group, hidden), BF),
            pltpu.VMEM((group, hidden), F32),
            pltpu.VMEM((rows, padded), BF),
            pltpu.VMEM((rows, padded), BF),
            pltpu.VMEM((rows, padded), BF),
            pltpu.VMEM((rows, padded), BF),
            pltpu.VMEM((rows, padded), BF),
            pltpu.VMEM((pairs, heads_lane * rows, rows), F32),
            pltpu.VMEM((rows, rows), F32),
            pltpu.VMEM((rows, width), F32),
            pltpu.VMEM((rows, width), F32),
            pltpu.VMEM((rows, LANES), F32),
            pltpu.VMEM((rows, width), F32),
            pltpu.VMEM((rows, width), F32),
            pltpu.VMEM((rows, width), F32),
            pltpu.VMEM((rows, width), F32),
            *bufs,
            *bufs,
            dma((4,)),
            dma((chunks,)),
            dma((chunks,)),
            dma((2, count)),
            dma((2, count)),
            dma((2, count)),
            dma((2, count)),
            dma((2, count)),
            dma((2, count)),
            dma((2, count)),
            dma((2, count)),
        ],
        compiler_params=pltpu.CompilerParams(
            collective_id=0, has_side_effects=True, vmem_limit_bytes=58 * 1024 * 1024
        ),
    )(tokens, lengths, w_qkv, w_out, w_up, up_bias[None], w_down, gains, biases, cotangent)


def greet(partner, peers):
    barrier = pltpu.get_barrier_semaphore()
    for place in [partner] + peers:
        pl.semaphore_signal(
            barrier,
            inc=1,
            device_id={"tensor": place},
            device_id_type=pl.DeviceIdType.MESH,
        )
    pl.semaphore_wait(barrier, 1 + len(peers))


def send(source, target, send_sem, recv_sem, place):
    copy = pltpu.make_async_remote_copy(
        src_ref=source,
        dst_ref=target,
        send_sem=send_sem,
        recv_sem=recv_sem,
        device_id={"tensor": place},
        device_id_type=pl.DeviceIdType.MESH,
    )
    copy.start()
    return copy


def gather_kernel(chips, rows, own_ref, out_ref, send_sem, recv_sem):
    me = lax.axis_index("tensor")
    core = lax.rem(me, 2)
    chip = me // 2
    partner = me + 1 - 2 * core
    peers = [lax.rem(chip + k, chips) * 2 + core for k in range(1, chips)]
    greet(partner, peers)

    def block(index):
        return out_ref.at[pl.ds(pl.multiple_of(index * rows, rows), rows)]

    across = [
        send(own_ref, block(me), send_sem.at[k], recv_sem.at[k], peer)
        for k, peer in enumerate(peers)
    ]
    beside = [send(own_ref, block(me), send_sem.at[chips - 1], recv_sem.at[chips - 1], partner)]
    out_ref[pl.ds(pl.multiple_of(me * rows, rows), rows)] = own_ref[...]
    for k, copy in enumerate(across):
        copy.wait_recv()
        origin = block(lax.rem(chip + chips - 1 - k, chips) * 2 + core)
        beside.append(send(origin, origin, send_sem.at[chips + k], recv_sem.at[chips + k], partner))
    for copy in across:
        copy.wait_send()
    for copy in beside:
        copy.wait()


def gather_rows(own, call=0):
    chips = lax.axis_size("tensor") // 2
    rows, width = own.shape
    return pl.pallas_call(
        functools.partial(gather_kernel, chips, rows),
        out_shape=jax.ShapeDtypeStruct((2 * chips * rows, width), own.dtype),
        in_specs=[pl.BlockSpec(memory_space=pltpu.VMEM)],
        out_specs=pl.BlockSpec(memory_space=pltpu.VMEM),
        scratch_shapes=[
            pltpu.SemaphoreType.DMA((2 * chips - 1,)),
            pltpu.SemaphoreType.DMA((2 * chips - 1,)),
        ],
        compiler_params=pltpu.CompilerParams(collective_id=call, has_side_effects=True),
    )(own)


def per_device(tokens, lengths, w_qkv, w_out, w_up, up_bias, w_down, gains, biases, cotangent):
    row_count, model_width = tokens.shape
    result, grad_in, normal_one, mixed, grad_proj, grad_resid_b, normal_two, grad_out, small = run_layers(
        tokens, lengths[0], w_qkv[0], w_out[0], w_up[0], up_bias[0], w_down[0], gains[0], biases[0], cotangent
    )
    owners = lax.axis_size(("dp", "tensor"))
    piece = model_width // owners

    def scatter_all(parts):
        return lax.psum_scatter(parts, ("dp", "tensor"), scatter_dimension=0).astype(jnp.float32)

    grad_wqkv = dot(normal_one, grad_proj, 0, 0)
    grad_wout = dot(mixed, grad_resid_b, 0, 0)
    grad_wout = scatter_all(grad_wout.astype(jnp.bfloat16).reshape(owners, piece, -1))
    qkv_width = grad_wqkv.shape[1]
    joined = jnp.concatenate([grad_wqkv.astype(jnp.bfloat16), small.T.astype(jnp.bfloat16)], axis=1)
    joined = joined.reshape(owners, piece, -1)
    inputs_dp = lax.all_gather(normal_two, "dp", axis=0, tiled=True)
    grads_dp = lax.all_gather(grad_out, "dp", axis=0, tiled=True)
    inputs_all = gather_rows(inputs_dp, 2)
    grads_all = gather_rows(grads_dp, 2)
    pre_all = dot(inputs_all, w_up[0]) + up_bias
    hidden_all, slope = gelu_both(pre_all)
    grad_all = dot(grads_all, w_down[0], 1, 1) * slope
    grad_up = dot(inputs_all, grad_all.astype(BF), 0, 0)
    grad_down = dot(hidden_all.astype(BF), grads_all, 0, 0)
    grad_up_bias = jnp.sum(grad_all, axis=0)
    joined = scatter_all(joined)
    grad_wqkv, small = joined[:, :qkv_width], joined[:, qkv_width:].T
    return (
        result[None],
        grad_in[None],
        grad_wqkv[None],
        grad_wout[None],
        small[None, :2],
        small[None, 2:],
        grad_up[None],
        grad_up_bias[None],
        grad_down[None],
    )


def solution(mesh):
    in_specs = (
        P(("dp", "tensor"), None),
        P(("dp", "tensor"), None, None),
        P("section", None, None),
        P("section", None, None),
        P("section", None, "tensor"),
        P("section", "tensor"),
        P("section", "tensor", None),
        P("section", None, None),
        P("section", None, None),
        P(("dp", "tensor"), None),
    )
    out_specs = (
        P("section", ("dp", "tensor"), None),
        P("section", ("dp", "tensor"), None),
        P("section", ("dp", "tensor"), None),
        P("section", ("dp", "tensor"), None),
        P("section", None, ("dp", "tensor")),
        P("section", None, ("dp", "tensor")),
        P("section", None, "tensor"),
        P("section", "tensor"),
        P("section", "tensor", None),
    )
    return jax.shard_map(
        per_device, mesh=mesh, in_specs=in_specs, out_specs=out_specs, check_vma=False
    )
```

```python
import functools
import math

import jax
import jax.numpy as jnp
from jax import lax
from jax.experimental import pallas as pl
from jax.experimental.pallas import tpu as pltpu
from jax.sharding import PartitionSpec as P

HEADS = 17
LANES = 128
EPSILON = 1e-05
GELU_SCALE = math.sqrt(2.0 / math.pi)
GELU_CUBIC = 0.044715
MESH = pl.DeviceIdType.MESH
BF = jnp.bfloat16
F32 = jnp.float32


def dot(left, right, left_dim=1, right_dim=0):
    return lax.dot_general(
        left, right, (((left_dim,), (right_dim,)), ((), ())), preferred_element_type=F32
    )


def norm_rows(values):
    centre = values - jnp.mean(values, axis=-1, keepdims=True)
    inverse = lax.rsqrt(jnp.mean(centre * centre, axis=-1, keepdims=True) + EPSILON)
    return (centre * inverse, inverse)


def norm_back(grad_normed, normed, inverse, gain):
    scaled = grad_normed * gain
    return (
        scaled
        - jnp.mean(scaled, axis=-1, keepdims=True)
        - normed * jnp.mean(scaled * normed, axis=-1, keepdims=True)
    ) * inverse


def gelu_both(values):
    square = values * values
    tangent = jnp.tanh(GELU_SCALE * values * (1.0 + GELU_CUBIC * square))
    raised = 0.5 * (1.0 + tangent)
    slope = raised + (0.5 * GELU_SCALE) * values * (1.0 - tangent * tangent) * (
        1.0 + 3.0 * GELU_CUBIC * square
    )
    return values * raised, slope


class Refs:
    def __init__(self, names, refs):
        self.__dict__.update(zip(names, refs, strict=True))


QUARTERS = ("o", "v", "q", "k")


def layers_kernel(sizes, names, *refs):
    r = Refs(names, refs)
    chips, chunks, groups, full, piece, slot = sizes
    sec = lax.axis_index("section")
    me = lax.axis_index("tensor")
    core = lax.rem(me, 2)
    chip = me // 2
    partner = me + 1 - 2 * core
    hops = chips - 1
    devices = 2 * chips
    up_chips = [lax.rem(chip + k, chips) for k in range(1, chips)]
    down_chips = [lax.rem(chip + chips - k, chips) for k in range(1, chips)]
    rows, width = r.tokens.shape
    part_rows = rows // chunks
    head_width = width // HEADS
    heads_lane = LANES // head_width
    pairs = -(-HEADS // heads_lane)
    scale = head_width ** (-0.5)
    place = lax.axis_index("dp") if full else 0
    home = place * (devices * rows)
    others = range(1, groups)

    loads = [
        pltpu.make_async_copy(src, dst, r.w_sem.at[i])
        for i, (src, dst) in enumerate(
            (
                (r.wqkv_hbm, r.wqkv),
                (r.wout_hbm, r.wout),
                (r.wup_hbm, r.wup),
                (r.wdn_hbm, r.wdn),
            )
        )
    ]
    for load in loads:
        load.start()
    barrier = pltpu.get_barrier_semaphore()
    friends = [{"section": 1 - sec}]
    if full:
        friends += [{"tensor": lax.rem(me + k, devices)} for k in range(1, devices)]
        friends += [{"dp": lax.rem(place + o, groups)} for o in others]
    else:
        friends += [{"tensor": partner}]
        friends += [{"tensor": c * 2 + core} for c in up_chips]
    for friend in friends:
        pl.semaphore_signal(barrier, inc=1, device_id=friend, device_id_type=MESH)

    def remote(src, dst, send_sem, recv_sem, where):
        return pltpu.make_async_remote_copy(
            src_ref=src,
            dst_ref=dst,
            send_sem=send_sem,
            recv_sem=recv_sem,
            device_id=where,
            device_id_type=MESH,
        )

    def span(first, size):
        return pl.ds(pl.multiple_of(first, 16), size)

    blocks, seqs = r.lengths.shape
    row_id = lax.broadcasted_iota(jnp.int32, (rows, rows), 0)
    col_id = lax.broadcasted_iota(jnp.int32, (rows, rows), 1)
    row_seg = jnp.zeros((rows, rows), jnp.int32)
    col_seg = jnp.zeros((rows, rows), jnp.int32)
    for b in range(blocks):
        end = b * (rows // blocks)
        for s in range(seqs):
            end = end + r.lengths[b, s]
            row_seg += (row_id >= end).astype(jnp.int32)
            col_seg += (col_id >= end).astype(jnp.int32)
    allowed = (row_seg == col_seg) & (col_id <= row_id)
    r.limit[...] = jnp.where(allowed, 0.0, -jnp.inf).astype(F32)
    lane = lax.broadcasted_iota(jnp.int32, (rows, LANES), 1)

    def stacked(tile):
        zero = jnp.zeros_like(tile)
        return jnp.concatenate(
            [jnp.where(lane // head_width == j, tile, zero) for j in range(heads_lane)], axis=0
        )

    def unstacked(tile):
        out = tile[:rows]
        for j in range(1, heads_lane):
            out = jnp.where(lane // head_width == j, tile[j * rows : (j + 1) * rows], out)
        return out

    def lanes(p):
        return slice(p * LANES, (p + 1) * LANES)

    pl.semaphore_wait(barrier, len(friends))
    drains = []

    class Gather:
        def __init__(self, buf, base, which, cuts):
            self.buf, self.base, self.which, self.cuts = buf, base, which, cuts
            self.size = rows // cuts

        def x_copy(self, ref, i, where):
            return remote(
                ref, ref, r.gx_send.at[self.which, i], r.gx_recv.at[self.which, i], where
            )

        def b_copy(self, ref, i):
            return remote(
                ref,
                ref,
                r.gb_send.at[self.which, i],
                r.gb_recv.at[self.which, i],
                {"tensor": partner},
            )

        def block(self, index, c):
            return self.buf.at[span(self.base + index * rows + c * self.size, self.size)]

        def whole(self, index):
            return self.buf.at[span(self.base + index * rows, rows)]

        def start(self):
            for c in range(self.cuts):
                for k in range(hops):
                    self.x_copy(
                        self.block(me, c), k * self.cuts + c, {"tensor": up_chips[k] * 2 + core}
                    ).start()
            self.b_copy(self.whole(me), hops * self.cuts).start()

        def forward(self, k, c):
            came = self.block(down_chips[k] * 2 + core, c)
            i = k * self.cuts + c
            self.x_copy(came, i, {"tensor": partner}).wait_recv()
            self.b_copy(came, i).start()

        def arrived(self, k, c):
            came = self.block(down_chips[k] * 2 + 1 - core, c)
            self.b_copy(came, k * self.cuts + c).wait_recv()

        def beside(self):
            self.b_copy(self.whole(partner), hops * self.cuts).wait_recv()

        def steps(self):
            return [(k, c) for c in range(self.cuts) for k in range(hops)]

        def forward_all(self):
            for k, c in self.steps():
                self.forward(k, c)

        def arrived_all(self):
            self.beside()
            for k, c in self.steps():
                self.arrived(k, c)

        def end(self):
            for i in range(hops * self.cuts):
                self.x_copy(self.block(me, 0), i, {"tensor": partner}).wait_send()
                self.b_copy(self.block(me, 0), i).wait_send()
            self.b_copy(self.whole(me), hops * self.cuts).wait_send()

    gather_x = Gather(r.x_all, home, 0, chunks)
    gather_g = Gather(r.g_all, home, 1, chunks)

    def dp_copy(buf, which, o, index):
        block = buf.at[span((index * devices + me) * rows, rows)]
        return remote(
            block,
            block,
            r.d_send.at[which, o - 1],
            r.d_recv.at[which, o - 1],
            {"dp": lax.rem(place + o, groups)},
        )

    def dp_start(buf, which):
        for o in others:
            dp_copy(buf, which, o, place).start()

    def dp_end(buf, which):
        for o in others:
            dp_copy(buf, which, o, place).wait_send()

    def dp_from(o):
        return lax.rem(place + groups - o, groups)

    def dp_gather(buf, which, o):
        base = dp_from(o) * (devices * rows)
        return Gather(buf, base, 2 + len(QUARTERS) + which * (groups - 1) + o - 1, 1)

    def dp_spread(buf, which, o):
        if o in others:
            dp_copy(buf, which, o, dp_from(o)).wait_recv()
            dp_gather(buf, which, o).start()


    def ffn_pass(gather, stage_one, stage_two, which, bufs, ready):
        besideb, acrossb = bufs
        order = [(k, c) for c in range(chunks) for k in range(hops)]
        chip_rows = [span(home + chip * 2 * rows, 2 * rows)]
        last = hops * chunks

        def both(k, c):
            theirs = down_chips[k] * 2 + 1 - core
            ours = down_chips[k] * 2 + core
            return [
                span(home + theirs * rows + c * part_rows, part_rows),
                span(home + ours * rows + c * part_rows, part_rows),
            ]

        def pair_copy(i, where):
            return remote(
                r.beside.at[where],
                besideb.at[where],
                r.sb_send.at[which, i],
                r.sb_recv.at[which, i],
                {"tensor": partner},
            )

        def across_copy(i, where, target):
            return remote(
                r.across.at[where],
                acrossb.at[where],
                r.sx_send.at[which, i],
                r.sx_recv.at[which, i],
                {"tensor": target},
            )

        if gather is not None:
            gather.beside()
            stage_one(chip_rows)
            if order:
                gather.forward(*order[0])

        def local():
            value = stage_two(chip_rows)
            theirs = jnp.where(core == 0, value[rows:], value[:rows])
            ours = jnp.where(core == 0, value[:rows], value[rows:])
            where = span(last * part_rows, rows)
            r.beside[where] = theirs.astype(BF)
            r.local_part[...] = ours
            pair_copy(last, where).start()

        for n, (k, c) in enumerate(order):
            i = k * chunks + c
            where = span(i * part_rows, part_rows)
            if gather is not None:
                gather.arrived(k, c)
                stage_one(both(k, c))
            value = stage_two(both(k, c))
            r.beside[where] = value[:part_rows].astype(BF)
            r.mine[where] = value[part_rows:].astype(BF)
            pair = pair_copy(i, where)
            pair.start()
            if gather is not None and n + 1 < len(order):
                gather.forward(*order[n + 1])
            if n == 0:
                local()
            pair.wait_recv()
            r.across[where] = (r.mine[where].astype(F32) + besideb[where].astype(F32)).astype(BF)
            across_copy(i, where, down_chips[k] * 2 + core).start()
        if not order:
            local()
        final = pair_copy(last, span(last * part_rows, rows))
        final.wait_recv()
        for c in range(chunks):
            here = slice(c * part_rows, (c + 1) * part_rows)
            total = r.local_part[here] + besideb[
                span(last * part_rows + c * part_rows, part_rows)
            ].astype(F32)
            for k in range(hops):
                i = k * chunks + c
                spot = span(i * part_rows, part_rows)
                across_copy(i, spot, partner).wait_recv()
                total = total + acrossb[spot].astype(F32)
            ready(c, here, total)
        final.wait_send()
        for k, c in order:
            i = k * chunks + c
            spot = span(i * part_rows, part_rows)
            pair_copy(i, spot).wait_send()
            across_copy(i, spot, partner).wait_send()

    def take(ref, spans):
        if len(spans) == 1:
            return ref[spans[0]]
        return jnp.concatenate([ref[s] for s in spans], axis=0)

    def put(ref, spans, value):
        size = value.shape[0] // len(spans)
        for n, s in enumerate(spans):
            ref[s] = value[n * size : (n + 1) * size].astype(ref.dtype)

    def up_stage(spans):
        pre = dot(take(r.x_all, spans), r.wup[...]) + r.upb[...]
        value, lean = gelu_both(pre)
        put(r.hid, spans, value)
        return lean

    def slope_stage(spans):
        put(r.slope, spans, up_stage(spans))

    def grad_stage(spans):
        put(r.slope, spans, dot(take(r.g_all, spans), r.wdn[...], 1, 1))

    def product(spans, value):
        value = value * take(r.slope, spans).astype(F32)
        put(r.slope, spans, value)
        if full:
            r.gupb[...] += jnp.sum(value, axis=0, keepdims=True)

    def up_pre_stage(spans):
        product(spans, up_stage(spans))

    def grad_pre_stage(spans):
        product(spans, dot(take(r.g_all, spans), r.wdn[...], 1, 1))

    def down_part(spans):
        return dot(take(r.hid, spans), r.wdn[...])

    def up_back(spans):
        return dot(take(r.slope, spans), r.wup[...], 1, 1)

    f_bufs = (r.f_besideb, r.f_acrossb)
    b_bufs = (r.b_besideb, r.b_acrossb)

    def result_ready(c, here, total):
        r.res[here] = (r.resid[here] + total + r.bias[5:6]).astype(BF)

    def y_result(c):
        here = slice(c * part_rows, (c + 1) * part_rows)
        return remote(
            r.res.at[here], r.lin.at[here], r.y_send.at[c], r.y_recv.at[c], {"section": 1 - sec}
        )

    def y_grad(c):
        here = slice(c * part_rows, (c + 1) * part_rows)
        arrive = r.g_all.at[span(home + me * rows + c * part_rows, part_rows)]
        return remote(
            r.gin.at[here], arrive, r.y_send.at[c], r.y_recv.at[c], {"section": 1 - sec}
        )

    def result_send(c, here, total):
        result_ready(c, here, total)
        y_result(c).start()

    def acc_ready(c, here, total):
        r.acc[here] = total

    own = span(home + me * rows, rows)
    if full:
        r.gupb[...] = jnp.zeros_like(r.gupb)

    @pl.when(sec == 1)
    def _():
        first_rows = pltpu.make_async_copy(r.cot, r.g_all.at[own], r.w_sem.at[4])
        first_rows.start()
        first_rows.wait()
        gather_g.start()
        if full:
            dp_start(r.g_all, 1)
        loads[3].wait()
        gather_g.beside()
        grad_stage([span(home + chip * 2 * rows, 2 * rows)])
        gather_g.forward_all()
        for k, c in gather_g.steps():
            gather_g.arrived(k, c)
        for k in range(hops):
            grad_stage([span(home + down_chips[k] * 2 * rows, 2 * rows)])
        gather_g.end()
        for c in range(chunks):
            y_result(c).wait_recv()

    @pl.when(sec == 0)
    def _():
        first_rows = pltpu.make_async_copy(r.tokens, r.lin, r.w_sem.at[4])
        first_rows.start()
        first_rows.wait()
        loads[3].wait()

    normed, inverse = norm_rows(r.lin[...].astype(F32))
    r.inv[:, 0:1] = inverse
    r.one[...] = (normed * r.gains[0:1] + r.bias[0:1]).astype(BF)
    loads[0].wait()
    proj = dot(r.one[...], r.wqkv[...])
    for ref, first, shift in ((r.q_s, 0, 1), (r.k_s, width, None), (r.v_s, 2 * width, 2)):
        value = proj[:, first : first + width]
        if shift is not None:
            value = value + r.bias[shift : shift + 1]
        ref[:, :width] = value.astype(BF)
        if ref.shape[1] > width:
            ref[:, width:] = jnp.zeros((rows, ref.shape[1] - width), BF)
    for p in range(pairs):
        r.probs[p] = dot(stacked(r.q_s[:, lanes(p)]), r.k_s[:, lanes(p)], 1, 1)
    limit = jnp.concatenate([r.limit[...]] * heads_lane, axis=0)
    for p in range(pairs):
        masked = r.probs[p] * scale + limit
        raised = jnp.exp(masked - jnp.max(masked, axis=-1, keepdims=True))
        r.probs[p] = raised / jnp.sum(raised, axis=-1, keepdims=True)
    for p in range(pairs):
        tile = unstacked(dot(r.probs[p].astype(BF), r.v_s[:, lanes(p)])).astype(BF)
        size = min(width - p * LANES, LANES)
        r.mix[:, p * LANES : p * LANES + size] = tile[:, :size]
    loads[1].wait()
    value = r.lin[...].astype(F32) + dot(r.mix[...], r.wout[...]) + r.bias[3:4]
    r.resid[...] = value
    normed, inverse = norm_rows(value)
    r.inv[:, 1:2] = inverse
    r.x_all[own] = (normed * r.gains[1:2] + r.bias[4:5]).astype(BF)
    gather_x.start()
    if full:
        dp_start(r.x_all, 0)
    loads[2].wait()

    spread = slot * groups

    def lhs_copy(i, t):
        lane_at = i * spread_lanes
        return remote(
            r.stage.at[span(t * rows, rows), lane_at : lane_at + spread_lanes],
            r.lhs.at[i, span(me * rows, rows)],
            r.l_send.at[i, t],
            r.l_recv.at[i, me],
            {"tensor": t},
        )

    spread_lanes = -(-spread // LANES) * LANES

    def select_columns():
        for k in range(devices):
            t = lax.rem(me + k, devices)
            values = [jnp.zeros((rows, spread_lanes), F32) for _ in range(2)]
            for first in range(0, width, 2 * LANES):
                size = min(2 * LANES, width - first)
                row = lax.broadcasted_iota(jnp.int32, (size, spread_lanes), 0) + first
                col = lax.broadcasted_iota(jnp.int32, (size, spread_lanes), 1)
                owner, inner = col // slot, col % slot
                hit = (row == (owner * devices + t) * piece + inner) & (inner < piece) & (owner < groups)
                chosen = jnp.where(hit, 1.0, 0.0).astype(BF)
                for i, ref in enumerate((r.one, r.mix)):
                    values[i] += dot(ref[:, first : first + size], chosen)
            for i, value in enumerate(values):
                if k == 0:
                    r.lhs[i, span(me * rows, rows)] = value.astype(BF)
                else:
                    lane_at = i * spread_lanes
                    r.stage[span(t * rows, rows), lane_at : lane_at + spread_lanes] = value.astype(BF)
                    lhs_copy(i, t).start()
        for k in range(1, devices):
            for i in range(2):
                lhs_copy(i, lax.rem(me + k, devices)).wait_send()

    def lhs_arrived():
        for k in range(1, devices):
            t = lax.rem(me + k, devices)
            for i in range(2):
                came = r.lhs.at[i, span(t * rows, rows)]
                remote(
                    came, came, r.l_send.at[i, t], r.l_recv.at[i, t], {"tensor": t}
                ).wait_recv()

    def dp_forward(buf, which, o):
        dp_gather(buf, which, o).forward_all()

    def dp_stage(buf, which, o, stage):
        dp_gather(buf, which, o).arrived_all()
        base = dp_from(o) * (devices * rows)

        @pl.loop(0, chips)
        def _(n):
            stage([span(base + n * 2 * rows, 2 * rows)])

    @pl.when(sec == 0)
    def _():
        ffn_pass(gather_x, slope_stage, down_part, 0, f_bufs, result_send)
        if full:
            select_columns()
            dp_spread(r.x_all, 0, 1)
            for o in others:
                dp_forward(r.x_all, 0, o)
                dp_spread(r.x_all, 0, o + 1)
                dp_stage(r.x_all, 0, o, slope_stage)
        for c in range(chunks):
            y_result(c).wait_send()
            y_grad(c).wait_recv()
        gather_g.start()
        if full:
            dp_start(r.g_all, 1)
        ffn_pass(gather_g, grad_pre_stage, up_back, 1, b_bufs, acc_ready)
        gather_g.end()

    @pl.when(sec == 1)
    def _():
        ffn_pass(gather_x, up_pre_stage, up_back, 1, b_bufs, acc_ready)

    gather_x.end()

    flow = r.g_all[own].astype(F32)
    grad_two = r.acc[...]
    residual = r.resid[...]
    normed = (residual - jnp.mean(residual, axis=-1, keepdims=True)) * r.inv[:, 1:2]
    value = flow + norm_back(grad_two, normed, r.inv[:, 1:2], r.gains[1:2])
    r.local_part[...] = value
    if full:
        right = {"o": r.r_o, "v": r.r_v, "q": r.r_q, "k": r.r_k}
        gathers = {u: Gather(right[u], 0, 2 + n, 1) for n, u in enumerate(QUARTERS)}
        mine = span(me * rows, rows)
    else:
        right = {"o": r.gres}
        mine = slice(0, rows)
    right["o"][mine] = value.astype(BF)
    if full:
        gathers["o"].start()
    r.small[1:2] = jnp.sum(normed * grad_two, axis=0, keepdims=True)
    r.small[5:6] = jnp.sum(value, axis=0, keepdims=True)
    r.small[6:7] = jnp.sum(grad_two, axis=0, keepdims=True)
    r.small[7:8] = jnp.sum(flow, axis=0, keepdims=True)
    r.gm_s[:, :width] = dot(right["o"][mine], r.wout[...], 1, 1).astype(BF)
    if r.gm_s.shape[1] > width:
        r.gm_s[:, width:] = jnp.zeros((rows, r.gm_s.shape[1] - width), BF)

    def ends(p):
        return p * LANES, min(width - p * LANES, LANES)

    for p in range(pairs):
        at, size = ends(p)
        gv = dot(r.probs[p].astype(BF), stacked(r.gm_s[:, lanes(p)]), 0, 0)
        r.small[4:5, at : at + size] = jnp.sum(gv, axis=0, keepdims=True)[:, :size]
        r.gproj[:, 2 * width + at : 2 * width + at + size] = gv.astype(BF)[:, :size]
        if full:
            right["v"][mine, at : at + size] = gv.astype(BF)[:, :size]
    if full:
        gathers["v"].start()
    for p in range(pairs):
        at, size = ends(p)
        weights = r.probs[p]
        grad_probs = dot(stacked(r.gm_s[:, lanes(p)]), r.v_s[:, lanes(p)], 1, 1)
        centre = jnp.sum(weights * grad_probs, axis=-1, keepdims=True)
        grad_scores = (weights * (grad_probs - centre) * scale).astype(BF)
        gq = unstacked(dot(grad_scores, r.k_s[:, lanes(p)]))
        gk = dot(grad_scores, stacked(r.q_s[:, lanes(p)]), 0, 0).astype(BF)
        r.small[3:4, at : at + size] = jnp.sum(gq, axis=0, keepdims=True)[:, :size]
        r.gproj[:, at : at + size] = gq.astype(BF)[:, :size]
        r.gk_s[:, at : at + LANES] = gk
        if full:
            right["q"][mine, at : at + size] = gq.astype(BF)[:, :size]
            right["k"][mine, at : at + size] = gk[:, :size]
    if full:
        gathers["o"].forward_all()
    r.gproj[:, width : 2 * width] = r.gk_s[:, :width]
    step = 5 * LANES
    whole = 3 * width // step
    rest = slice(whole * step, 3 * width)
    r.acc[0:rows] = dot(r.gproj[:, rest], r.wqkv[:, rest], 1, 1)

    @pl.loop(0, whole)
    def _(n):
        cols = pl.ds(pl.multiple_of(n * step, LANES), step)
        r.acc[0:rows] += dot(r.gproj[:, cols], r.wqkv[:, cols], 1, 1)

    grad_one = r.acc[0:rows]
    inflow = r.lin[...].astype(F32)
    normed = (inflow - jnp.mean(inflow, axis=-1, keepdims=True)) * r.inv[:, 0:1]
    r.gin[...] = (
        r.local_part[...] + norm_back(grad_one, normed, r.inv[:, 0:1], r.gains[0:1])
    ).astype(BF)

    def late_result():
        ffn_pass(None, None, down_part, 0, f_bufs, result_ready)

    @pl.when(sec == 1)
    def _():
        for c in range(chunks):
            y_grad(c).start()
        if full:
            dp_spread(r.x_all, 0, 1)
            select_columns()
        else:
            late_result()
            for c in range(chunks):
                y_grad(c).wait_send()

    r.small[0:1] = jnp.sum(normed * grad_one, axis=0, keepdims=True)
    r.small[2:3] = jnp.sum(grad_one, axis=0, keepdims=True)
    if not full:
        return

    def small_copy(i, src, dst, k, where):
        return remote(src, dst, r.m_send.at[i, k], r.m_recv.at[i, k], where)

    def small_t(k):
        return small_copy(
            0, r.small, r.small_all.at[k], k, {"tensor": lax.rem(me + k, devices)}
        )

    def small_d(o):
        return small_copy(
            1, r.small_sum, r.small_dp.at[o], o, {"dp": lax.rem(place + o, groups)}
        )

    def small_one():
        for k in range(1, devices):
            small_t(k).start()

    def small_two():
        total = r.small[...]
        for k in range(1, devices):
            small_t(k).wait_recv()
            total = total + r.small_all[k]
        r.small_sum[...] = total
        for o in others:
            small_d(o).start()

    def small_three():
        total = r.small_sum[...]
        for o in others:
            small_d(o).wait_recv()
            total = total + r.small_dp[o]
        r.small_out[...] = total

    strip = groups * slot
    stack = min(len(QUARTERS), width // strip)
    lanes_all = r.came.shape[1]

    def sum_at(n, target, size):
        lane_at = n // stack * lanes_all
        return span(n % stack * strip + target * slot, size), slice(lane_at, lane_at + width)

    def sum_rows(n, target):
        lane_at = n // stack * lanes_all
        return r.wqkv.at[sum_at(n, target, slot)[0], lane_at : lane_at + lanes_all]

    def came_rows(n, index):
        return r.came.at[span((n * (groups + 1) + index) * slot, slot)]

    def partial(n):
        u = QUARTERS[n]
        left = r.lhs[1 if u == "o" else 0, :, :spread]
        r.wqkv[sum_at(n, 0, strip)] = dot(left, right[u][...], 0, 0).astype(BF)

    def chain_copy(n, way, target):
        step = 1 - 2 * way
        index = target if way == 0 else jnp.where(target == place - 1, groups, target)
        return remote(
            sum_rows(n, target),
            came_rows(n, index),
            r.c_send.at[n * 2 + way, target],
            r.c_recv.at[n * 2 + way, target],
            {"dp": place + step},
        )

    def chain_came(n, way, target):
        index = jnp.where(target == place, groups, target) if way == 1 else target
        ref = came_rows(n, index)
        return (
            remote(
                ref,
                ref,
                r.c_send.at[n * 2 + way, target],
                r.c_recv.at[n * 2 + way, target],
                {"dp": place},
            ),
            span((n * (groups + 1) + index) * slot, slot),
        )

    def chain_step(n, o):
        for way in range(2):
            target = place + o if way == 0 else place - o
            inside = target < groups if way == 0 else target >= 0
            behind = place > 0 if way == 0 else place < groups - 1

            @pl.when(inside)
            def _():
                @pl.when(behind)
                def _():
                    wait, where = chain_came(n, way, target)
                    wait.wait_recv()
                    spot = sum_at(n, target, slot)
                    r.wqkv[spot] = (r.wqkv[spot].astype(F32) + r.came[where, 0:width].astype(F32)).astype(BF)

                chain_copy(n, way, target).start()

    def chain_end(n):
        for o in others:
            for way in range(2):
                target = place + o if way == 0 else place - o

                @pl.when(target < groups if way == 0 else target >= 0)
                def _():
                    chain_copy(n, way, target).wait_send()

    def chain_final(n):
        r.acc[0:slot] = r.wqkv[sum_at(n, place, slot)].astype(F32)
        for way in range(2):

            @pl.when(place > 0 if way == 0 else place < groups - 1)
            def _():
                wait, where = chain_came(n, way, place)
                wait.wait_recv()
                r.acc[0:slot] += r.came[where, 0:width].astype(F32)

        value = r.acc[0:piece]
        u = QUARTERS[n]
        if u == "o":
            r.gw_out[...] = value.astype(BF)
        else:
            first = {"q": 0, "k": 1, "v": 2}[u] * width
            r.gw_qkv[:, first : first + width] = value.astype(BF)

    tile = 256
    tiles = []
    for left, rhs, out in ((r.hid, r.g_all, r.gdn_hbm), (r.x_all, r.slope, r.gup_hbm)):
        for first in range(0, left.shape[1], tile):
            tiles.append((left, rhs, out, first, min(tile, left.shape[1] - first)))

    def tile_copy(n):
        _, rhs, out, first, size = tiles[n]
        half = n % 2 * tile
        return pltpu.make_async_copy(
            r.stage.at[half : half + size, 0 : rhs.shape[1]],
            out.at[first : first + size],
            r.t_sem.at[n],
        )

    def tile_step(n):
        left, rhs, out, first, size = tiles[n]
        if n >= 2:
            tile_copy(n - 2).wait()
        half = n % 2 * tile
        value = dot(left[:, first : first + size], rhs[...], 0, 0)
        r.stage[half : half + size, 0 : rhs.shape[1]] = value.astype(BF)
        tile_copy(n).start()

    def second(body):
        @pl.when(sec == 1)
        def _():
            body()

    def late_x(o):
        dp_forward(r.x_all, 0, o)
        dp_spread(r.x_all, 0, o + 1)
        dp_stage(r.x_all, 0, o, slope_stage)

    def g_forward(o):
        if o in others:
            dp_forward(r.g_all, 1, o)

    def g_spread(o):
        dp_spread(r.g_all, 1, o)

    def g_stage(o):
        dp_stage(r.g_all, 1, o, grad_pre_stage)

    def late_all():
        for o in others:
            late_x(o)

    call = functools.partial
    works = [[] for _ in QUARTERS]
    works[0] = [
        lambda: (gathers["v"].forward_all(), g_spread(1), small_one()),
        lambda: second(late_result),
    ]
    works[1] = [
        lambda: (gathers["q"].forward_all(), g_spread(2), small_two()),
        lambda: (g_forward(1), g_spread(3)),
        lambda: second(late_all),
    ]
    works[2] = [lambda: (g_forward(2), gathers["k"].start())]
    for o in others:
        works[2].append(call(g_stage, o))
        if o + 2 in others:
            works[2].append(call(g_forward, o + 2))
            works[2].append(call(g_spread, o + 3))
    works[2].append(gathers["k"].forward_all)
    works[3] = [call(tile_step, n) for n in range(len(tiles))]

    gathers["q"].start()
    lhs_arrived()
    for n, u in enumerate(QUARTERS):
        gathers[u].arrived_all()
        partial(n)
        work, total = list(works[n]), len(works[n])
        for done, o in enumerate(reversed(others)):
            chain_step(n, o)
            while work and (total - len(work)) * (groups - 1) < (done + 1) * total:
                work.pop(0)()
        while work:
            work.pop(0)()
        if n > 0:
            chain_final(n - 1)
    small_three()
    chain_final(len(QUARTERS) - 1)

    for n in range(max(len(tiles) - 2, 0), len(tiles)):
        tile_copy(n).wait()
    for n in range(len(QUARTERS)):
        chain_end(n)
    for u in QUARTERS:
        gathers[u].end()
    for which, buf in enumerate((r.x_all, r.g_all)):
        dp_end(buf, which)
        for o in others:
            dp_gather(buf, which, o).end()
    for k in range(1, devices):
        small_t(k).wait_send()
    for o in others:
        small_d(o).wait_send()

    @pl.when(sec == 1)
    def _():
        for c in range(chunks):
            y_grad(c).wait_send()


def run_layers(tokens, lengths, w_qkv, w_out, w_up, up_bias, w_down, gains, biases, cotangent):
    devices = lax.axis_size("tensor")
    chips = devices // 2
    hops = chips - 1
    rows, width = tokens.shape
    chunks = 2 if rows % 32 == 0 else 1
    part_rows = rows // chunks
    hidden = w_up.shape[1]
    padded = -(-width // LANES) * LANES
    heads_lane = LANES // (width // HEADS)
    pairs = -(-HEADS // heads_lane)
    groups = lax.axis_size("dp")
    full = groups * devices * rows * (width + hidden) * 4 <= 20 * 2**20
    piece = width // (groups * devices)
    slot = -(-piece // 16) * 16
    if not full:
        groups = 1
    group = devices * rows
    moved = max(hops * chunks * part_rows, 16)
    shape = jax.ShapeDtypeStruct
    vmem = pl.BlockSpec(memory_space=pltpu.VMEM)
    smem = pl.BlockSpec(memory_space=pltpu.SMEM)
    hbm = pl.BlockSpec(memory_space=pl.ANY)
    dma = pltpu.SemaphoreType.DMA
    v = pltpu.VMEM
    count = hops * chunks + 1
    inputs = {
        "tokens": (tokens, hbm),
        "lengths": (lengths, smem),
        "wqkv_hbm": (w_qkv, hbm),
        "wout_hbm": (w_out, hbm),
        "wup_hbm": (w_up, hbm),
        "upb": (up_bias[None], vmem),
        "wdn_hbm": (w_down, hbm),
        "gains": (gains, vmem),
        "bias": (biases, vmem),
        "cot": (cotangent, hbm),
    }
    outputs = {"res": (shape((rows, width), BF), vmem), "gin": (shape((rows, width), BF), vmem)}
    scratch = {
        "wqkv": v(w_qkv.shape, BF),
        "wout": v(w_out.shape, BF),
        "wup": v(w_up.shape, BF),
        "wdn": v(w_down.shape, BF),
        "lin": v((rows, width), BF),
        "x_all": v((groups * group, width), BF),
        "g_all": v((groups * group, width), BF),
        "hid": v((groups * group, hidden), BF),
        "slope": v((groups * group, hidden), BF),
        "q_s": v((rows, padded), BF),
        "k_s": v((rows, padded), BF),
        "v_s": v((rows, padded), BF),
        "gm_s": v((rows, padded), BF),
        "gk_s": v((rows, padded), BF),
        "probs": v((pairs, heads_lane * rows, rows), F32),
        "limit": v((rows, rows), F32),
        "inv": v((rows, LANES), F32),
        "resid": v((rows, width), F32),
        "acc": v((max(rows, slot), width), F32),
        "local_part": v((rows, width), F32),
        "beside": v((moved + rows, width), BF),
        "mine": v((moved, width), BF),
        "across": v((moved, width), BF),
        "f_besideb": v((moved + rows, width), BF),
        "b_besideb": v((moved + rows, width), BF),
        "f_acrossb": v((moved, width), BF),
        "b_acrossb": v((moved, width), BF),
        "w_sem": dma((5,)),
        "y_send": dma((chunks,)),
        "y_recv": dma((chunks,)),
    }
    gathers = 2
    if full:
        spread_lanes = -(-groups * slot // LANES) * LANES
        gathers += len(QUARTERS) + 2 * (groups - 1)
        outputs["gw_qkv"] = (shape((piece, 3 * width), BF), vmem)
        outputs["gw_out"] = (shape((piece, width), BF), vmem)
        outputs["gup_hbm"] = (shape((width, hidden), BF), hbm)
        outputs["gdn_hbm"] = (shape((hidden, width), BF), hbm)
        outputs["gupb"] = (shape((1, hidden), F32), vmem)
        outputs["small_out"] = (shape((8, width), F32), vmem)
        scratch |= {
            "one": v((rows, width), BF),
            "mix": v((rows, width), BF),
            "gproj": v((rows, 3 * width), BF),
            "r_o": v((group, width), BF),
            "r_v": v((group, width), BF),
            "r_q": v((group, width), BF),
            "r_k": v((group, width), BF),
            "lhs": v((2, group, spread_lanes), BF),
            "came": v((len(QUARTERS) * (groups + 1) * slot, padded), BF),
            "stage": v((max(group, 512), max(width, hidden, 2 * spread_lanes)), BF),
            "small": v((8, width), F32),
            "small_sum": v((8, width), F32),
            "small_all": v((devices, 8, width), F32),
            "small_dp": v((groups, 8, width), F32),
            "d_send": dma((2, max(groups - 1, 1))),
            "d_recv": dma((2, max(groups - 1, 1))),
            "l_send": dma((2, devices)),
            "l_recv": dma((2, devices)),
            "m_send": dma((2, max(devices, groups))),
            "m_recv": dma((2, max(devices, groups))),
            "c_send": dma((2 * len(QUARTERS), groups)),
            "c_recv": dma((2 * len(QUARTERS), groups)),
            "t_sem": dma((-(-width // 256) + -(-hidden // 256),)),
        }
    else:
        outputs["one"] = (shape((rows, width), BF), vmem)
        outputs["mix"] = (shape((rows, width), BF), vmem)
        outputs["gproj"] = (shape((rows, 3 * width), BF), vmem)
        outputs["gres"] = (shape((rows, width), BF), vmem)
        outputs["small"] = (shape((8, width), F32), vmem)
        outputs["x_all"] = (shape((group, width), BF), vmem)
        outputs["g_all"] = (shape((group, width), BF), vmem)
        del scratch["x_all"], scratch["g_all"]
    scratch |= {
        "gx_send": dma((gathers, count)),
        "gx_recv": dma((gathers, count)),
        "gb_send": dma((gathers, count)),
        "gb_recv": dma((gathers, count)),
        "sx_send": dma((2, count)),
        "sx_recv": dma((2, count)),
        "sb_send": dma((2, count)),
        "sb_recv": dma((2, count)),
    }
    names = (*inputs, *outputs, *scratch)
    sizes = (chips, chunks, groups, full, piece, slot)
    results = pl.pallas_call(
        functools.partial(layers_kernel, sizes, names),
        out_shape=tuple(o[0] for o in outputs.values()),
        in_specs=[i[1] for i in inputs.values()],
        out_specs=tuple(o[1] for o in outputs.values()),
        scratch_shapes=list(scratch.values()),
        compiler_params=pltpu.CompilerParams(
            collective_id=0, has_side_effects=True, vmem_limit_bytes=61 * 2**20
        ),
    )(*(i[0] for i in inputs.values()))
    return full, dict(zip(outputs, results, strict=True))


def per_device(tokens, lengths, w_qkv, w_out, w_up, up_bias, w_down, gains, biases, cotangent):
    width = tokens.shape[1]
    full, made = run_layers(
        tokens,
        lengths[0],
        w_qkv[0],
        w_out[0],
        w_up[0],
        up_bias[0],
        w_down[0],
        gains[0],
        biases[0],
        cotangent,
    )
    owners = lax.axis_size(("dp", "tensor"))
    piece = width // owners
    if full:
        grad_wqkv, grad_wout = made["gw_qkv"].astype(F32), made["gw_out"].astype(F32)
        grad_up, grad_down = made["gup_hbm"].astype(F32), made["gdn_hbm"].astype(F32)
        grad_up_bias = made["gupb"][0]
        owner = lax.axis_index(("dp", "tensor"))
        small = lax.dynamic_slice_in_dim(made["small_out"], owner * piece, piece, 1)
    else:

        def scatter_all(parts):
            parts = parts.astype(BF).reshape(owners, piece, -1)
            return lax.psum_scatter(parts, ("dp", "tensor"), scatter_dimension=0).astype(F32)

        grad_wqkv = dot(made["one"], made["gproj"], 0, 0)
        grad_wout = scatter_all(dot(made["mix"], made["gres"], 0, 0))
        joined = scatter_all(jnp.concatenate([grad_wqkv, made["small"].T], axis=1))
        grad_wqkv, small = joined[:, : 3 * width], joined[:, 3 * width :].T
        inputs_all = lax.all_gather(made["x_all"], "dp", axis=0, tiled=True)
        grads_all = lax.all_gather(made["g_all"], "dp", axis=0, tiled=True)
        hidden_all, slope = gelu_both(dot(inputs_all, w_up[0]) + up_bias)
        grad_all = dot(grads_all, w_down[0], 1, 1) * slope
        grad_up = dot(inputs_all, grad_all.astype(BF), 0, 0)
        grad_down = dot(hidden_all.astype(BF), grads_all, 0, 0)
        grad_up_bias = jnp.sum(grad_all, axis=0)
    return (
        made["res"][None],
        made["gin"][None],
        grad_wqkv[None],
        grad_wout[None],
        small[None, :2],
        small[None, 2:],
        grad_up[None],
        grad_up_bias[None],
        grad_down[None],
    )


def solution(mesh):
    in_specs = (
        P(("dp", "tensor"), None),
        P(("dp", "tensor"), None, None),
        P("section", None, None),
        P("section", None, None),
        P("section", None, "tensor"),
        P("section", "tensor"),
        P("section", "tensor", None),
        P("section", None, None),
        P("section", None, None),
        P(("dp", "tensor"), None),
    )
    out_specs = (
        P("section", ("dp", "tensor"), None),
        P("section", ("dp", "tensor"), None),
        P("section", ("dp", "tensor"), None),
        P("section", ("dp", "tensor"), None),
        P("section", None, ("dp", "tensor")),
        P("section", None, ("dp", "tensor")),
        P("section", None, "tensor"),
        P("section", "tensor"),
        P("section", "tensor", None),
    )
    return jax.shard_map(
        per_device, mesh=mesh, in_specs=in_specs, out_specs=out_specs, check_vma=False
    )
```

```python
import functools
import math

import jax
import jax.numpy as jnp
from jax import lax
from jax.experimental import pallas as pl
from jax.experimental.pallas import tpu as pltpu
from jax.sharding import PartitionSpec as P

HEADS = 17
LANES = 128
EPSILON = 1e-05
GELU_SCALE = math.sqrt(2.0 / math.pi)
GELU_CUBIC = 0.044715
MESH = pl.DeviceIdType.MESH
BF = jnp.bfloat16
F32 = jnp.float32


def dot(left, right, left_dim=1, right_dim=0):
    return lax.dot_general(
        left, right, (((left_dim,), (right_dim,)), ((), ())), preferred_element_type=F32
    )


def norm_rows(values):
    centre = values - jnp.mean(values, axis=-1, keepdims=True)
    inverse = lax.rsqrt(jnp.mean(centre * centre, axis=-1, keepdims=True) + EPSILON)
    return (centre * inverse, inverse)


def norm_back(grad_normed, normed, inverse, gain):
    scaled = grad_normed * gain
    return (
        scaled
        - jnp.mean(scaled, axis=-1, keepdims=True)
        - normed * jnp.mean(scaled * normed, axis=-1, keepdims=True)
    ) * inverse


def gelu_both(values):
    square = values * values
    tangent = jnp.tanh(GELU_SCALE * values * (1.0 + GELU_CUBIC * square))
    raised = 0.5 * (1.0 + tangent)
    slope = raised + (0.5 * GELU_SCALE) * values * (1.0 - tangent * tangent) * (
        1.0 + 3.0 * GELU_CUBIC * square
    )
    return values * raised, slope


class Refs:
    def __init__(self, names, refs):
        self.__dict__.update(zip(names, refs, strict=True))


QUARTERS = ("o", "v", "q", "k")


def layers_kernel(sizes, names, *refs):
    r = Refs(names, refs)
    chips, chunks, groups, full, piece, slot = sizes
    sec = lax.axis_index("section")
    me = lax.axis_index("tensor")
    core = lax.rem(me, 2)
    chip = me // 2
    partner = me + 1 - 2 * core
    hops = chips - 1
    devices = 2 * chips
    up_chips = [lax.rem(chip + k, chips) for k in range(1, chips)]
    down_chips = [lax.rem(chip + chips - k, chips) for k in range(1, chips)]
    rows, width = r.lin.shape
    part_rows = rows // chunks
    head_width = width // HEADS
    heads_lane = LANES // head_width
    pairs = -(-HEADS // heads_lane)
    scale = head_width ** (-0.5)
    place = lax.axis_index("dp") if full else 0
    home = place * (devices * rows)
    others = range(1, groups)

    loads = [
        pltpu.make_async_copy(src, dst, r.w_sem.at[i])
        for i, (src, dst) in enumerate(
            (
                (r.wqkv_hbm, r.wqkv),
                (r.wout_hbm, r.wout),
                (r.wup_hbm, r.wup),
                (r.wdn_hbm, r.wdn),
            )
        )
    ]
    for load in loads:
        load.start()
    barrier = pltpu.get_barrier_semaphore()
    friends = [{"section": 1 - sec}]
    if full:
        friends += [{"tensor": lax.rem(me + k, devices)} for k in range(1, devices)]
        friends += [{"dp": lax.rem(place + o, groups)} for o in others]
    else:
        friends += [{"tensor": partner}]
        friends += [{"tensor": c * 2 + core} for c in up_chips]
    for friend in friends:
        pl.semaphore_signal(barrier, inc=1, device_id=friend, device_id_type=MESH)

    def remote(src, dst, send_sem, recv_sem, where):
        return pltpu.make_async_remote_copy(
            src_ref=src,
            dst_ref=dst,
            send_sem=send_sem,
            recv_sem=recv_sem,
            device_id=where,
            device_id_type=MESH,
        )

    def span(first, size):
        return pl.ds(pl.multiple_of(first, 16), size)

    blocks, seqs = r.lengths.shape
    row_id = lax.broadcasted_iota(jnp.int32, (rows, rows), 0)
    col_id = lax.broadcasted_iota(jnp.int32, (rows, rows), 1)
    row_seg = jnp.zeros((rows, rows), jnp.int32)
    col_seg = jnp.zeros((rows, rows), jnp.int32)
    for b in range(blocks):
        end = b * (rows // blocks)
        for s in range(seqs):
            end = end + r.lengths[b, s]
            row_seg += (row_id >= end).astype(jnp.int32)
            col_seg += (col_id >= end).astype(jnp.int32)
    allowed = (row_seg == col_seg) & (col_id <= row_id)
    r.limit[...] = jnp.where(allowed, 0.0, -jnp.inf).astype(F32)
    lane = lax.broadcasted_iota(jnp.int32, (rows, LANES), 1)

    def stacked(tile):
        zero = jnp.zeros_like(tile)
        return jnp.concatenate(
            [jnp.where(lane // head_width == j, tile, zero) for j in range(heads_lane)], axis=0
        )

    def unstacked(tile):
        out = tile[:rows]
        for j in range(1, heads_lane):
            out = jnp.where(lane // head_width == j, tile[j * rows : (j + 1) * rows], out)
        return out

    def lanes(p):
        return slice(p * LANES, (p + 1) * LANES)

    pl.semaphore_wait(barrier, len(friends))
    drains = []

    class Gather:
        def __init__(self, buf, base, which, cuts):
            self.buf, self.base, self.which, self.cuts = buf, base, which, cuts
            self.size = rows // cuts

        def x_copy(self, ref, i, where):
            return remote(
                ref, ref, r.gx_send.at[self.which, i], r.gx_recv.at[self.which, i], where
            )

        def b_copy(self, ref, i):
            return remote(
                ref,
                ref,
                r.gb_send.at[self.which, i],
                r.gb_recv.at[self.which, i],
                {"tensor": partner},
            )

        def block(self, index, c):
            return self.buf.at[span(self.base + index * rows + c * self.size, self.size)]

        def whole(self, index):
            return self.buf.at[span(self.base + index * rows, rows)]

        def start(self):
            for c in range(self.cuts):
                for k in range(hops):
                    self.x_copy(
                        self.block(me, c), k * self.cuts + c, {"tensor": up_chips[k] * 2 + core}
                    ).start()
            self.b_copy(self.whole(me), hops * self.cuts).start()

        def forward(self, k, c):
            came = self.block(down_chips[k] * 2 + core, c)
            i = k * self.cuts + c
            self.x_copy(came, i, {"tensor": partner}).wait_recv()
            self.b_copy(came, i).start()

        def arrived(self, k, c):
            came = self.block(down_chips[k] * 2 + 1 - core, c)
            self.b_copy(came, k * self.cuts + c).wait_recv()

        def beside(self):
            self.b_copy(self.whole(partner), hops * self.cuts).wait_recv()

        def steps(self):
            return [(k, c) for c in range(self.cuts) for k in range(hops)]

        def forward_all(self):
            for k, c in self.steps():
                self.forward(k, c)

        def arrived_all(self):
            self.beside()
            for k, c in self.steps():
                self.arrived(k, c)

        def end(self):
            for i in range(hops * self.cuts):
                self.x_copy(self.block(me, 0), i, {"tensor": partner}).wait_send()
                self.b_copy(self.block(me, 0), i).wait_send()
            self.b_copy(self.whole(me), hops * self.cuts).wait_send()

    gather_x = Gather(r.x_all, home, 0, chunks)
    gather_g = Gather(r.g_all, home, 1, chunks)

    def dp_copy(buf, which, o, index):
        block = buf.at[span((index * devices + me) * rows, rows)]
        return remote(
            block,
            block,
            r.d_send.at[which, o - 1],
            r.d_recv.at[which, o - 1],
            {"dp": lax.rem(place + o, groups)},
        )

    def dp_start(buf, which):
        for o in others:
            dp_copy(buf, which, o, place).start()

    def dp_end(buf, which):
        for o in others:
            dp_copy(buf, which, o, place).wait_send()

    def dp_from(o):
        return lax.rem(place + groups - o, groups)

    def dp_gather(buf, which, o):
        base = dp_from(o) * (devices * rows)
        return Gather(buf, base, 2 + len(QUARTERS) + which * (groups - 1) + o - 1, 1)

    def dp_spread(buf, which, o):
        if o in others:
            dp_copy(buf, which, o, dp_from(o)).wait_recv()
            dp_gather(buf, which, o).start()


    def ffn_pass(gather, stage_one, stage_two, which, bufs, ready):
        besideb, acrossb = bufs
        order = [(k, c) for c in range(chunks) for k in range(hops)]
        chip_rows = [span(home + chip * 2 * rows, 2 * rows)]
        last = hops * chunks

        def both(k, c):
            theirs = down_chips[k] * 2 + 1 - core
            ours = down_chips[k] * 2 + core
            return [
                span(home + theirs * rows + c * part_rows, part_rows),
                span(home + ours * rows + c * part_rows, part_rows),
            ]

        def pair_copy(i, where):
            return remote(
                r.beside.at[where],
                besideb.at[where],
                r.sb_send.at[which, i],
                r.sb_recv.at[which, i],
                {"tensor": partner},
            )

        def across_copy(i, where, target):
            return remote(
                r.across.at[where],
                acrossb.at[where],
                r.sx_send.at[which, i],
                r.sx_recv.at[which, i],
                {"tensor": target},
            )

        if gather is not None:
            gather.beside()
            stage_one(chip_rows)
            if order:
                gather.forward(*order[0])

        def local():
            value = stage_two(chip_rows)
            theirs = jnp.where(core == 0, value[rows:], value[:rows])
            ours = jnp.where(core == 0, value[:rows], value[rows:])
            where = span(last * part_rows, rows)
            r.beside[where] = theirs.astype(BF)
            r.local_part[...] = ours
            pair_copy(last, where).start()

        for n, (k, c) in enumerate(order):
            i = k * chunks + c
            where = span(i * part_rows, part_rows)
            if gather is not None:
                gather.arrived(k, c)
                stage_one(both(k, c))
            value = stage_two(both(k, c))
            r.beside[where] = value[:part_rows].astype(BF)
            r.mine[where] = value[part_rows:].astype(BF)
            pair = pair_copy(i, where)
            pair.start()
            if gather is not None and n + 1 < len(order):
                gather.forward(*order[n + 1])
            if n == 0:
                local()
            pair.wait_recv()
            r.across[where] = (r.mine[where].astype(F32) + besideb[where].astype(F32)).astype(BF)
            across_copy(i, where, down_chips[k] * 2 + core).start()
        if not order:
            local()
        final = pair_copy(last, span(last * part_rows, rows))
        final.wait_recv()
        for c in range(chunks):
            here = slice(c * part_rows, (c + 1) * part_rows)
            total = r.local_part[here] + besideb[
                span(last * part_rows + c * part_rows, part_rows)
            ].astype(F32)
            for k in range(hops):
                i = k * chunks + c
                spot = span(i * part_rows, part_rows)
                across_copy(i, spot, partner).wait_recv()
                total = total + acrossb[spot].astype(F32)
            ready(c, here, total)
        final.wait_send()
        for k, c in order:
            i = k * chunks + c
            spot = span(i * part_rows, part_rows)
            pair_copy(i, spot).wait_send()
            across_copy(i, spot, partner).wait_send()

    def take(ref, spans):
        if len(spans) == 1:
            return ref[spans[0]]
        return jnp.concatenate([ref[s] for s in spans], axis=0)

    def put(ref, spans, value):
        size = value.shape[0] // len(spans)
        for n, s in enumerate(spans):
            ref[s] = value[n * size : (n + 1) * size].astype(ref.dtype)

    def up_stage(spans):
        pre = dot(take(r.x_all, spans), r.wup[...]) + r.upb[...]
        value, lean = gelu_both(pre)
        put(r.hid, spans, value)
        return lean

    def slope_stage(spans):
        put(r.slope, spans, up_stage(spans))

    def grad_stage(spans):
        put(r.slope, spans, dot(take(r.g_all, spans), r.wdn[...], 1, 1))

    def product(spans, value):
        value = value * take(r.slope, spans).astype(F32)
        put(r.slope, spans, value)
        if full:
            r.gupb[...] += jnp.sum(value, axis=0, keepdims=True)

    def up_pre_stage(spans):
        product(spans, up_stage(spans))

    def grad_pre_stage(spans):
        product(spans, dot(take(r.g_all, spans), r.wdn[...], 1, 1))

    def down_part(spans):
        return dot(take(r.hid, spans), r.wdn[...])

    def up_back(spans):
        return dot(take(r.slope, spans), r.wup[...], 1, 1)

    f_bufs = (r.f_besideb, r.f_acrossb)
    b_bufs = (r.b_besideb, r.b_acrossb)

    def result_ready(c, here, total):
        r.res[here] = (r.resid[here] + total + r.bias[5]).astype(BF)

    def y_result(c):
        here = slice(c * part_rows, (c + 1) * part_rows)
        return remote(
            r.res.at[here], r.lin.at[here], r.y_send.at[c], r.y_recv.at[c], {"section": 1 - sec}
        )

    def y_grad(c):
        here = slice(c * part_rows, (c + 1) * part_rows)
        arrive = r.g_all.at[span(home + me * rows + c * part_rows, part_rows)]
        return remote(
            r.gin.at[here], arrive, r.y_send.at[c], r.y_recv.at[c], {"section": 1 - sec}
        )

    def result_send(c, here, total):
        result_ready(c, here, total)
        y_result(c).start()

    def acc_ready(c, here, total):
        r.acc[here] = total

    def bring(source, ref, where):
        turned = source.shape[0] != rows
        landing = r.hid.at[0:width, 0:rows] if turned else ref.at[where]
        copy = pltpu.make_async_copy(source, landing, r.w_sem.at[4])
        copy.start()
        copy.wait()
        if turned:
            ref[where] = dot((row_id == col_id).astype(BF), r.hid[0:width, 0:rows], 1, 1).astype(BF)

    own = span(home + me * rows, rows)
    if full:
        r.gupb[...] = jnp.zeros_like(r.gupb)

    @pl.when(sec == 1)
    def _():
        bring(r.cot, r.g_all, own)
        gather_g.start()
        if full:
            dp_start(r.g_all, 1)
        loads[3].wait()
        gather_g.beside()
        grad_stage([span(home + chip * 2 * rows, 2 * rows)])
        gather_g.forward_all()
        for k, c in gather_g.steps():
            gather_g.arrived(k, c)
        for k in range(hops):
            grad_stage([span(home + down_chips[k] * 2 * rows, 2 * rows)])
        gather_g.end()
        for c in range(chunks):
            y_result(c).wait_recv()

    @pl.when(sec == 0)
    def _():
        bring(r.tokens, r.lin, slice(0, rows))
        loads[3].wait()

    normed, inverse = norm_rows(r.lin[...].astype(F32))
    r.inv[:, 0:1] = inverse
    r.one[...] = (normed * r.gains[0:1] + r.bias[0]).astype(BF)
    loads[0].wait()
    proj = dot(r.one[...], r.wqkv[...])
    for ref, first, shift in ((r.q_s, 0, 1), (r.k_s, width, None), (r.v_s, 2 * width, 2)):
        value = proj[:, first : first + width]
        if shift is not None:
            value = value + r.bias[shift]
        ref[:, :width] = value.astype(BF)
        if ref.shape[1] > width:
            ref[:, width:] = jnp.zeros((rows, ref.shape[1] - width), BF)
    for p in range(pairs):
        r.probs[p] = dot(stacked(r.q_s[:, lanes(p)]), r.k_s[:, lanes(p)], 1, 1)
    limit = jnp.concatenate([r.limit[...]] * heads_lane, axis=0)
    for p in range(pairs):
        masked = r.probs[p] * scale + limit
        raised = jnp.exp(masked - jnp.max(masked, axis=-1, keepdims=True))
        r.probs[p] = raised / jnp.sum(raised, axis=-1, keepdims=True)
    for p in range(pairs):
        tile = unstacked(dot(r.probs[p].astype(BF), r.v_s[:, lanes(p)])).astype(BF)
        size = min(width - p * LANES, LANES)
        r.mix[:, p * LANES : p * LANES + size] = tile[:, :size]
    loads[1].wait()
    value = r.lin[...].astype(F32) + dot(r.mix[...], r.wout[...]) + r.bias[3]
    r.resid[...] = value
    normed, inverse = norm_rows(value)
    r.inv[:, 1:2] = inverse
    r.x_all[own] = (normed * r.gains[1:2] + r.bias[4]).astype(BF)
    gather_x.start()
    if full:
        dp_start(r.x_all, 0)
    loads[2].wait()

    spread = slot * groups

    def lhs_copy(i, t):
        lane_at = i * spread_lanes
        return remote(
            r.stage.at[span(t * rows, rows), lane_at : lane_at + spread_lanes],
            r.lhs.at[i, span(me * rows, rows)],
            r.l_send.at[i, t],
            r.l_recv.at[i, me],
            {"tensor": t},
        )

    spread_lanes = -(-spread // LANES) * LANES

    def select_columns():
        col = lax.broadcasted_iota(jnp.int32, (1, spread_lanes), 1)
        owner, inner = col // slot, col % slot
        wanted = jnp.where(
            (inner < piece) & (owner < groups), owner * (devices * piece) + inner, -2 * width
        )
        for k in range(devices):
            t = lax.rem(me + k, devices)
            values = [jnp.zeros((rows, spread_lanes), F32) for _ in range(2)]
            for first in range(0, width, 2 * LANES):
                size = min(2 * LANES, width - first)
                row = lax.broadcasted_iota(jnp.int32, (size, spread_lanes), 0) + first
                chosen = jnp.where(row == wanted + t * piece, 1.0, 0.0).astype(BF)
                for i, ref in enumerate((r.one, r.mix)):
                    values[i] += dot(ref[:, first : first + size], chosen)
            for i, value in enumerate(values):
                if k == 0:
                    r.lhs[i, span(me * rows, rows)] = value.astype(BF)
                else:
                    lane_at = i * spread_lanes
                    r.stage[span(t * rows, rows), lane_at : lane_at + spread_lanes] = value.astype(BF)
                    lhs_copy(i, t).start()
        for k in range(1, devices):
            for i in range(2):
                lhs_copy(i, lax.rem(me + k, devices)).wait_send()

    def lhs_arrived():
        for k in range(1, devices):
            t = lax.rem(me + k, devices)
            for i in range(2):
                came = r.lhs.at[i, span(t * rows, rows)]
                remote(
                    came, came, r.l_send.at[i, t], r.l_recv.at[i, t], {"tensor": t}
                ).wait_recv()

    def dp_forward(buf, which, o):
        dp_gather(buf, which, o).forward_all()

    def dp_stage(buf, which, o, stage):
        dp_gather(buf, which, o).arrived_all()
        base = dp_from(o) * (devices * rows)

        @pl.loop(0, chips)
        def _(n):
            stage([span(base + n * 2 * rows, 2 * rows)])

    @pl.when(sec == 0)
    def _():
        ffn_pass(gather_x, slope_stage, down_part, 0, f_bufs, result_send)
        if full:
            select_columns()
            dp_spread(r.x_all, 0, 1)
            for o in others:
                dp_forward(r.x_all, 0, o)
                dp_spread(r.x_all, 0, o + 1)
                dp_stage(r.x_all, 0, o, slope_stage)
        for c in range(chunks):
            y_result(c).wait_send()
            y_grad(c).wait_recv()
        gather_g.start()
        if full:
            dp_start(r.g_all, 1)
        ffn_pass(gather_g, grad_pre_stage, up_back, 1, b_bufs, acc_ready)
        gather_g.end()

    @pl.when(sec == 1)
    def _():
        ffn_pass(gather_x, up_pre_stage, up_back, 1, b_bufs, acc_ready)

    gather_x.end()

    flow = r.g_all[own].astype(F32)
    grad_two = r.acc[...]
    residual = r.resid[...]
    normed = (residual - jnp.mean(residual, axis=-1, keepdims=True)) * r.inv[:, 1:2]
    value = flow + norm_back(grad_two, normed, r.inv[:, 1:2], r.gains[1:2])
    r.local_part[...] = value
    if full:
        right = {"o": r.r_o, "v": r.r_v, "q": r.r_q, "k": r.r_k}
        gathers = {u: Gather(right[u], 0, 2 + n, 1) for n, u in enumerate(QUARTERS)}
        mine = span(me * rows, rows)
    else:
        right = {"o": r.gres}
        mine = slice(0, rows)
    right["o"][mine] = value.astype(BF)
    if full:
        gathers["o"].start()
    r.small[1:2] = jnp.sum(normed * grad_two, axis=0, keepdims=True)
    r.small[5:6] = jnp.sum(value, axis=0, keepdims=True)
    r.small[6:7] = jnp.sum(grad_two, axis=0, keepdims=True)
    r.small[7:8] = jnp.sum(flow, axis=0, keepdims=True)
    r.gm_s[:, :width] = dot(right["o"][mine], r.wout[...], 1, 1).astype(BF)
    if r.gm_s.shape[1] > width:
        r.gm_s[:, width:] = jnp.zeros((rows, r.gm_s.shape[1] - width), BF)

    def ends(p):
        return p * LANES, min(width - p * LANES, LANES)

    for p in range(pairs):
        at, size = ends(p)
        gv = dot(r.probs[p].astype(BF), stacked(r.gm_s[:, lanes(p)]), 0, 0)
        r.small[4:5, at : at + size] = jnp.sum(gv, axis=0, keepdims=True)[:, :size]
        r.gproj[:, 2 * width + at : 2 * width + at + size] = gv.astype(BF)[:, :size]
        if full:
            right["v"][mine, at : at + size] = gv.astype(BF)[:, :size]
    if full:
        gathers["v"].start()
    for p in range(pairs):
        at, size = ends(p)
        weights = r.probs[p]
        grad_probs = dot(stacked(r.gm_s[:, lanes(p)]), r.v_s[:, lanes(p)], 1, 1)
        centre = jnp.sum(weights * grad_probs, axis=-1, keepdims=True)
        grad_scores = (weights * (grad_probs - centre) * scale).astype(BF)
        gq = unstacked(dot(grad_scores, r.k_s[:, lanes(p)]))
        gk = dot(grad_scores, stacked(r.q_s[:, lanes(p)]), 0, 0).astype(BF)
        r.small[3:4, at : at + size] = jnp.sum(gq, axis=0, keepdims=True)[:, :size]
        r.gproj[:, at : at + size] = gq.astype(BF)[:, :size]
        r.gk_s[:, at : at + LANES] = gk
        if full:
            right["q"][mine, at : at + size] = gq.astype(BF)[:, :size]
            right["k"][mine, at : at + size] = gk[:, :size]
    if full:
        gathers["o"].forward_all()
    r.gproj[:, width : 2 * width] = r.gk_s[:, :width]
    step = 5 * LANES
    whole = 3 * width // step
    rest = slice(whole * step, 3 * width)
    r.acc[0:rows] = dot(r.gproj[:, rest], r.wqkv[:, rest], 1, 1)

    @pl.loop(0, whole)
    def _(n):
        cols = pl.ds(pl.multiple_of(n * step, LANES), step)
        r.acc[0:rows] += dot(r.gproj[:, cols], r.wqkv[:, cols], 1, 1)

    grad_one = r.acc[0:rows]
    inflow = r.lin[...].astype(F32)
    normed = (inflow - jnp.mean(inflow, axis=-1, keepdims=True)) * r.inv[:, 0:1]
    r.gin[...] = (
        r.local_part[...] + norm_back(grad_one, normed, r.inv[:, 0:1], r.gains[0:1])
    ).astype(BF)

    def late_result():
        ffn_pass(None, None, down_part, 0, f_bufs, result_ready)

    @pl.when(sec == 1)
    def _():
        for c in range(chunks):
            y_grad(c).start()
        if full:
            dp_spread(r.x_all, 0, 1)
            select_columns()
        else:
            late_result()
            for c in range(chunks):
                y_grad(c).wait_send()

    r.small[0:1] = jnp.sum(normed * grad_one, axis=0, keepdims=True)
    r.small[2:3] = jnp.sum(grad_one, axis=0, keepdims=True)
    if not full:
        return

    def small_copy(i, src, dst, k, where):
        return remote(src, dst, r.m_send.at[i, k], r.m_recv.at[i, k], where)

    def small_t(k):
        return small_copy(
            0, r.small, r.small_all.at[k], k, {"tensor": lax.rem(me + k, devices)}
        )

    def small_d(o):
        return small_copy(
            1, r.small_sum, r.small_dp.at[o], o, {"dp": lax.rem(place + o, groups)}
        )

    def small_one():
        for k in range(1, devices):
            small_t(k).start()

    def small_two():
        total = r.small[...]
        for k in range(1, devices):
            small_t(k).wait_recv()
            total = total + r.small_all[k]
        r.small_sum[...] = total
        for o in others:
            small_d(o).start()

    def small_three():
        total = r.small_sum[...]
        for o in others:
            small_d(o).wait_recv()
            total = total + r.small_dp[o]
        r.small_out[...] = total

    strip = groups * slot
    stack = min(len(QUARTERS), width // strip)
    lanes_all = r.came.shape[1]

    def sum_at(n, target, size):
        lane_at = n // stack * lanes_all
        return span(n % stack * strip + target * slot, size), slice(lane_at, lane_at + width)

    def sum_rows(n, target):
        lane_at = n // stack * lanes_all
        return r.wqkv.at[sum_at(n, target, slot)[0], lane_at : lane_at + lanes_all]

    def came_rows(n, index):
        return r.came.at[span((n * (groups + 1) + index) * slot, slot)]

    def partial(n):
        u = QUARTERS[n]
        left = r.lhs[1 if u == "o" else 0, :, :spread]
        r.wqkv[sum_at(n, 0, strip)] = dot(left, right[u][...], 0, 0).astype(BF)

    def chain_copy(n, way, target):
        step = 1 - 2 * way
        index = target if way == 0 else jnp.where(target == place - 1, groups, target)
        return remote(
            sum_rows(n, target),
            came_rows(n, index),
            r.c_send.at[n * 2 + way, target],
            r.c_recv.at[n * 2 + way, target],
            {"dp": place + step},
        )

    def chain_came(n, way, target):
        index = jnp.where(target == place, groups, target) if way == 1 else target
        ref = came_rows(n, index)
        return (
            remote(
                ref,
                ref,
                r.c_send.at[n * 2 + way, target],
                r.c_recv.at[n * 2 + way, target],
                {"dp": place},
            ),
            span((n * (groups + 1) + index) * slot, slot),
        )

    def chain_step(n, o):
        for way in range(2):
            target = place + o if way == 0 else place - o
            inside = target < groups if way == 0 else target >= 0
            behind = place > 0 if way == 0 else place < groups - 1

            @pl.when(inside)
            def _():
                @pl.when(behind)
                def _():
                    wait, where = chain_came(n, way, target)
                    wait.wait_recv()
                    spot = sum_at(n, target, slot)
                    r.wqkv[spot] = (r.wqkv[spot].astype(F32) + r.came[where, 0:width].astype(F32)).astype(BF)

                chain_copy(n, way, target).start()

    def chain_end(n):
        for o in others:
            for way in range(2):
                target = place + o if way == 0 else place - o

                @pl.when(target < groups if way == 0 else target >= 0)
                def _():
                    chain_copy(n, way, target).wait_send()

    def chain_final(n):
        r.acc[0:slot] = r.wqkv[sum_at(n, place, slot)].astype(F32)
        for way in range(2):

            @pl.when(place > 0 if way == 0 else place < groups - 1)
            def _():
                wait, where = chain_came(n, way, place)
                wait.wait_recv()
                r.acc[0:slot] += r.came[where, 0:width].astype(F32)

        value = r.acc[0:piece]
        u = QUARTERS[n]
        if u == "o":
            r.gw_out[...] = value.astype(BF)
        else:
            first = {"q": 0, "k": 1, "v": 2}[u] * width
            r.gw_qkv[:, first : first + width] = value.astype(BF)

    tile = 256
    tiles = []
    for left, rhs, out in ((r.hid, r.g_all, r.gdn_hbm), (r.x_all, r.slope, r.gup_hbm)):
        for first in range(0, left.shape[1], tile):
            tiles.append((left, rhs, out, first, min(tile, left.shape[1] - first)))

    def tile_copy(n):
        _, rhs, out, first, size = tiles[n]
        half = n % 2 * tile
        return pltpu.make_async_copy(
            r.stage.at[half : half + size, 0 : rhs.shape[1]],
            out.at[first : first + size],
            r.t_sem.at[n],
        )

    def tile_step(n):
        left, rhs, out, first, size = tiles[n]
        if n >= 2:
            tile_copy(n - 2).wait()
        half = n % 2 * tile
        value = dot(left[:, first : first + size], rhs[...], 0, 0)
        r.stage[half : half + size, 0 : rhs.shape[1]] = value.astype(BF)
        tile_copy(n).start()

    def second(body):
        @pl.when(sec == 1)
        def _():
            body()

    def late_x(o):
        dp_forward(r.x_all, 0, o)
        dp_spread(r.x_all, 0, o + 1)
        dp_stage(r.x_all, 0, o, slope_stage)

    def g_forward(o):
        if o in others:
            dp_forward(r.g_all, 1, o)

    def g_spread(o):
        dp_spread(r.g_all, 1, o)

    def g_stage(o):
        dp_stage(r.g_all, 1, o, grad_pre_stage)

    def late_all():
        for o in others:
            late_x(o)

    call = functools.partial
    works = [[] for _ in QUARTERS]
    works[0] = [
        lambda: (gathers["v"].forward_all(), g_spread(1), small_one()),
        lambda: second(late_result),
    ]
    works[1] = [
        lambda: (gathers["q"].forward_all(), g_spread(2), small_two()),
        lambda: (g_forward(1), g_spread(3)),
        lambda: second(late_all),
    ]
    works[2] = [lambda: (g_forward(2), gathers["k"].start())]
    for o in others:
        works[2].append(call(g_stage, o))
        if o + 2 in others:
            works[2].append(call(g_forward, o + 2))
            works[2].append(call(g_spread, o + 3))
    early = len(tiles) * 2 // 5
    works[2] += [call(tile_step, n) for n in range(early)]
    works[2].append(gathers["k"].forward_all)
    works[3] = [call(tile_step, n) for n in range(early, len(tiles))]

    gathers["q"].start()
    lhs_arrived()
    for n, u in enumerate(QUARTERS):
        gathers[u].arrived_all()
        partial(n)
        work, total = list(works[n]), len(works[n])
        for done, o in enumerate(reversed(others)):
            chain_step(n, o)
            while work and (total - len(work)) * (groups - 1) < (done + 1) * total:
                work.pop(0)()
        while work:
            work.pop(0)()
        if n > 0:
            chain_final(n - 1)
    small_three()
    chain_final(len(QUARTERS) - 1)

    for n in range(max(len(tiles) - 2, 0), len(tiles)):
        tile_copy(n).wait()
    for n in range(len(QUARTERS)):
        chain_end(n)
    for u in QUARTERS:
        gathers[u].end()
    for which, buf in enumerate((r.x_all, r.g_all)):
        dp_end(buf, which)
        for o in others:
            dp_gather(buf, which, o).end()
    for k in range(1, devices):
        small_t(k).wait_send()
    for o in others:
        small_d(o).wait_send()

    @pl.when(sec == 1)
    def _():
        for c in range(chunks):
            y_grad(c).wait_send()


def run_layers(tokens, lengths, w_qkv, w_out, w_up, up_bias, w_down, gains, biases, cotangent):
    devices = lax.axis_size("tensor")
    chips = devices // 2
    hops = chips - 1
    rows, width = tokens.shape
    chunks = 2 if rows % 32 == 0 else 1
    part_rows = rows // chunks
    hidden = w_up.shape[1]
    padded = -(-width // LANES) * LANES
    heads_lane = LANES // (width // HEADS)
    pairs = -(-HEADS // heads_lane)
    groups = lax.axis_size("dp")
    full = groups * devices * rows * (width + hidden) * 4 <= 20 * 2**20
    piece = width // (groups * devices)
    slot = -(-piece // 16) * 16
    if not full:
        groups = 1
    group = devices * rows
    moved = max(hops * chunks * part_rows, 16)
    turned = rows % LANES == 0 and rows != width and groups * group >= width and hidden >= rows
    shape = jax.ShapeDtypeStruct
    vmem = pl.BlockSpec(memory_space=pltpu.VMEM)
    smem = pl.BlockSpec(memory_space=pltpu.SMEM)
    hbm = pl.BlockSpec(memory_space=pl.ANY)
    dma = pltpu.SemaphoreType.DMA
    v = pltpu.VMEM
    count = hops * chunks + 1
    inputs = {
        "tokens": (tokens.T if turned else tokens, hbm),
        "lengths": (lengths, smem),
        "wqkv_hbm": (w_qkv, hbm),
        "wout_hbm": (w_out, hbm),
        "wup_hbm": (w_up, hbm),
        "upb": (up_bias[None], vmem),
        "wdn_hbm": (w_down, hbm),
        "gains": (gains, vmem),
        "bias": (biases[:, None], vmem),
        "cot": (cotangent.T if turned else cotangent, hbm),
    }
    outputs = {"res": (shape((rows, width), BF), vmem), "gin": (shape((rows, width), BF), vmem)}
    scratch = {
        "wqkv": v(w_qkv.shape, BF),
        "wout": v(w_out.shape, BF),
        "wup": v(w_up.shape, BF),
        "wdn": v(w_down.shape, BF),
        "lin": v((rows, width), BF),
        "x_all": v((groups * group, width), BF),
        "g_all": v((groups * group, width), BF),
        "hid": v((groups * group, hidden), BF),
        "slope": v((groups * group, hidden), BF),
        "q_s": v((rows, padded), BF),
        "k_s": v((rows, padded), BF),
        "v_s": v((rows, padded), BF),
        "gm_s": v((rows, padded), BF),
        "gk_s": v((rows, padded), BF),
        "probs": v((pairs, heads_lane * rows, rows), F32),
        "limit": v((rows, rows), F32),
        "inv": v((rows, LANES), F32),
        "resid": v((rows, width), F32),
        "acc": v((max(rows, slot), width), F32),
        "local_part": v((rows, width), F32),
        "beside": v((moved + rows, width), BF),
        "mine": v((moved, width), BF),
        "across": v((moved, width), BF),
        "f_besideb": v((moved + rows, width), BF),
        "b_besideb": v((moved + rows, width), BF),
        "f_acrossb": v((moved, width), BF),
        "b_acrossb": v((moved, width), BF),
        "w_sem": dma((5,)),
        "y_send": dma((chunks,)),
        "y_recv": dma((chunks,)),
    }
    gathers = 2
    if full:
        spread_lanes = -(-groups * slot // LANES) * LANES
        gathers += len(QUARTERS) + 2 * (groups - 1)
        outputs["gw_qkv"] = (shape((piece, 3 * width), BF), vmem)
        outputs["gw_out"] = (shape((piece, width), BF), vmem)
        outputs["gup_hbm"] = (shape((width, hidden), BF), hbm)
        outputs["gdn_hbm"] = (shape((hidden, width), BF), hbm)
        outputs["gupb"] = (shape((1, hidden), F32), vmem)
        outputs["small_out"] = (shape((8, width), F32), vmem)
        scratch |= {
            "one": v((rows, width), BF),
            "mix": v((rows, width), BF),
            "gproj": v((rows, 3 * width), BF),
            "r_o": v((group, width), BF),
            "r_v": v((group, width), BF),
            "r_q": v((group, width), BF),
            "r_k": v((group, width), BF),
            "lhs": v((2, group, spread_lanes), BF),
            "came": v((len(QUARTERS) * (groups + 1) * slot, padded), BF),
            "stage": v((max(group, 512), max(width, hidden, 2 * spread_lanes)), BF),
            "small": v((8, width), F32),
            "small_sum": v((8, width), F32),
            "small_all": v((devices, 8, width), F32),
            "small_dp": v((groups, 8, width), F32),
            "d_send": dma((2, max(groups - 1, 1))),
            "d_recv": dma((2, max(groups - 1, 1))),
            "l_send": dma((2, devices)),
            "l_recv": dma((2, devices)),
            "m_send": dma((2, max(devices, groups))),
            "m_recv": dma((2, max(devices, groups))),
            "c_send": dma((2 * len(QUARTERS), groups)),
            "c_recv": dma((2 * len(QUARTERS), groups)),
            "t_sem": dma((-(-width // 256) + -(-hidden // 256),)),
        }
    else:
        outputs["one"] = (shape((rows, width), BF), vmem)
        outputs["mix"] = (shape((rows, width), BF), vmem)
        outputs["gproj"] = (shape((rows, 3 * width), BF), vmem)
        outputs["gres"] = (shape((rows, width), BF), vmem)
        outputs["small"] = (shape((8, width), F32), vmem)
        outputs["x_all"] = (shape((group, width), BF), vmem)
        outputs["g_all"] = (shape((group, width), BF), vmem)
        del scratch["x_all"], scratch["g_all"]
    scratch |= {
        "gx_send": dma((gathers, count)),
        "gx_recv": dma((gathers, count)),
        "gb_send": dma((gathers, count)),
        "gb_recv": dma((gathers, count)),
        "sx_send": dma((2, count)),
        "sx_recv": dma((2, count)),
        "sb_send": dma((2, count)),
        "sb_recv": dma((2, count)),
    }
    names = (*inputs, *outputs, *scratch)
    sizes = (chips, chunks, groups, full, piece, slot)
    results = pl.pallas_call(
        functools.partial(layers_kernel, sizes, names),
        out_shape=tuple(o[0] for o in outputs.values()),
        in_specs=[i[1] for i in inputs.values()],
        out_specs=tuple(o[1] for o in outputs.values()),
        scratch_shapes=list(scratch.values()),
        compiler_params=pltpu.CompilerParams(
            collective_id=0, has_side_effects=True, vmem_limit_bytes=61 * 2**20
        ),
    )(*(i[0] for i in inputs.values()))
    return full, dict(zip(outputs, results, strict=True))


def per_device(tokens, lengths, w_qkv, w_out, w_up, up_bias, w_down, gains, biases, cotangent):
    width = tokens.shape[1]
    full, made = run_layers(
        tokens,
        lengths[0],
        w_qkv[0],
        w_out[0],
        w_up[0],
        up_bias[0],
        w_down[0],
        gains[0],
        biases[0],
        cotangent,
    )
    owners = lax.axis_size(("dp", "tensor"))
    piece = width // owners
    if full:
        grad_wqkv, grad_wout = made["gw_qkv"].astype(F32), made["gw_out"].astype(F32)
        grad_up, grad_down = made["gup_hbm"].astype(F32), made["gdn_hbm"].astype(F32)
        grad_up_bias = made["gupb"][0]
        owner = lax.axis_index(("dp", "tensor"))
        small = lax.dynamic_slice_in_dim(made["small_out"], owner * piece, piece, 1)
    else:

        def scatter_all(parts):
            parts = parts.astype(BF).reshape(owners, piece, -1)
            return lax.psum_scatter(parts, ("dp", "tensor"), scatter_dimension=0).astype(F32)

        grad_wqkv = dot(made["one"], made["gproj"], 0, 0)
        grad_wout = scatter_all(dot(made["mix"], made["gres"], 0, 0))
        joined = scatter_all(jnp.concatenate([grad_wqkv, made["small"].T], axis=1))
        grad_wqkv, small = joined[:, : 3 * width], joined[:, 3 * width :].T
        inputs_all = lax.all_gather(made["x_all"], "dp", axis=0, tiled=True)
        grads_all = lax.all_gather(made["g_all"], "dp", axis=0, tiled=True)
        hidden_all, slope = gelu_both(dot(inputs_all, w_up[0]) + up_bias)
        grad_all = dot(grads_all, w_down[0], 1, 1) * slope
        grad_up = dot(inputs_all, grad_all.astype(BF), 0, 0)
        grad_down = dot(hidden_all.astype(BF), grads_all, 0, 0)
        grad_up_bias = jnp.sum(grad_all, axis=0)
    return (
        made["res"][None],
        made["gin"][None],
        grad_wqkv[None],
        grad_wout[None],
        small[None, :2],
        small[None, 2:],
        grad_up[None],
        grad_up_bias[None],
        grad_down[None],
    )


def solution(mesh):
    in_specs = (
        P(("dp", "tensor"), None),
        P(("dp", "tensor"), None, None),
        P("section", None, None),
        P("section", None, None),
        P("section", None, "tensor"),
        P("section", "tensor"),
        P("section", "tensor", None),
        P("section", None, None),
        P("section", None, None),
        P(("dp", "tensor"), None),
    )
    out_specs = (
        P("section", ("dp", "tensor"), None),
        P("section", ("dp", "tensor"), None),
        P("section", ("dp", "tensor"), None),
        P("section", ("dp", "tensor"), None),
        P("section", None, ("dp", "tensor")),
        P("section", None, ("dp", "tensor")),
        P("section", None, "tensor"),
        P("section", "tensor"),
        P("section", "tensor", None),
    )
    return jax.shard_map(
        per_device, mesh=mesh, in_specs=in_specs, out_specs=out_specs, check_vma=False
    )
```
